256 devices in a mesh: gen: 8 (over z_lo, core), user: 16 (over x, y), cand: 2 (over z_hi).
Axes of the slice: x: 4, y: 4, z: 8 (z_hi: 2, z_lo: 4; z = z_hi * 4 + z_lo), core: 2. Of those that a mesh axis runs over, the one named last changes fastest.
Arguments:
- states: bfloat16 [16384, 4096], P(('user', 'cand')), may hold values from -6 to 6
- norm_gain: float32 [4096], replicated, may hold values from 0.1 to 1.9
- gate_weight: bfloat16 [4096, 7168], P('user', 'gen'), may hold values from -0.09375 to 0.09375
- up_weight: bfloat16 [4096, 7168], P('user', 'gen'), may hold values from -0.09375 to 0.09375
- down_weight: bfloat16 [7168, 4096], P('gen', 'user'), may hold values from -0.0625 to 0.0625
- proj_weight: bfloat16 [4096, 1024], P('gen'), may hold values from -0.09375 to 0.09375
- private_rows: bfloat16 [32768, 1024], P(('gen', 'user')), may hold values from -6 to 6
- enc_weight: bfloat16 [1024, 1024], replicated, may hold values from -0.1875 to 0.1875
- user_ids: int32 [32768], P(('gen', 'user')), may hold values from 0 to 31
Outputs:
- votes: float32 [16, 2, 128], P(None, 'cand')
The draws below stay inside these ranges and needn't reach their ends.
Inputs may be any that keep to these rules, and one draw needn't show every extreme that they name: `user_ids`: a user is a pair of a block of 256 rows and a slot; no user has rows in two blocks.
All inputs are finite; a program needn't handle non-finite values.
Results may differ from the reference program's by a relative error of at most 0.0025.
Values may be sent and summed in bfloat16 or wider, within the bound.
No kernel may reach another device: no remote copies, remote signals or barrier semaphores. Data moves between devices by JAX's collectives and lax.ppermute only.
A program may use at most 128 MiB of HBM per device.

```python
import jax
import jax.numpy as jnp
from jax import lax

D = 4096
FF = 7168
EMB = 1024
STEPS = 4
CAP = 8
CG = 128
ROW_DEV = 256
USERS_DEV = 32
CANDS = 4096
TOKENS = 16384
ROWS = 32768
N_USER = 16
N_CAND = 2


def with_ends(array, key, least, largest):
    index_at = [jax.random.randint(jax.random.fold_in(key, axis), (), 0, length) for axis, length in enumerate(array.shape)]
    widest = array.shape.index(max(array.shape))
    neighbour = index_at[:widest] + [(index_at[widest] + 1) % array.shape[widest]] + index_at[widest + 1:]
    return array.at[tuple(index_at)].set(least).at[tuple(neighbour)].set(largest)


def block_scale(key, shape, pieces, low, largest):
    factor_of = 1.0
    for position, shards_of in pieces:
        heights = jax.random.uniform(jax.random.fold_in(jax.random.fold_in(key, 6), position), (shards_of,), jnp.float32, low / len(pieces), largest / len(pieces))
        factor_of = factor_of * jnp.repeat(jnp.exp(heights), shape[position] // shards_of).reshape((-1,) + (1,) * (len(shape) - 1 - position))
    return factor_of


def normal_values(stream_key, shape, spread, most, cuts=(), kind=jnp.bfloat16):
    gain = block_scale(stream_key, shape, cuts, -0.22, 0.18) if cuts else 1.0
    array = jax.random.normal(stream_key, shape, jnp.float32) * spread * gain
    return jnp.minimum(jnp.maximum(array, -most), most).astype(kind)


def setup_inputs(seed: int = 0) -> dict:
    streams_of = jax.random.split(jax.random.key(seed), 10)
    return {
        "states": normal_values(streams_of[0], (TOKENS, D), 1.0, 6.0, ((0, 32),)),
        "norm_gain": jnp.clip(1.0 + 0.18 * jax.random.normal(streams_of[1], (D,), jnp.float32), 0.1, 1.9),
        "gate_weight": normal_values(streams_of[2], (D, FF), D ** -0.5, 0.09375, ((0, 16), (1, 8))),
        "up_weight": normal_values(streams_of[3], (D, FF), D ** -0.5, 0.09375, ((0, 16), (1, 8))),
        "down_weight": normal_values(streams_of[4], (FF, D), FF ** -0.5, 0.0625, ((0, 8), (1, 16))),
        "proj_weight": normal_values(streams_of[5], (D, EMB), D ** -0.5, 0.09375, ((0, 8),)),
        "private_rows": normal_values(streams_of[6], (ROWS, EMB), 1.0, 6.0, ((0, 128),)),
        "enc_weight": normal_values(streams_of[7], (EMB, EMB), EMB ** -0.5, 0.1875),
        "user_ids": with_ends(jax.random.randint(streams_of[8], (ROWS,), 0, USERS_DEV), jax.random.fold_in(streams_of[8], 1), 0, USERS_DEV - 1).astype(jnp.int32),
    }


def unit_rows(matrix):
    return (matrix * lax.rsqrt(lax.optimization_barrier(jnp.sum(matrix * matrix, axis=1, keepdims=True)) + 1e-06)).astype(jnp.bfloat16)

def reference(states, norm_gain, gate_weight, up_weight, down_weight, proj_weight, private_rows, enc_weight, user_ids):
    group_tokens = CG * STEPS

    def layer_block(block):
        values = block.astype(jnp.float32)
        normed = (values * lax.rsqrt(lax.optimization_barrier(jnp.mean(values * values, axis=1, keepdims=True)) + 1e-05) * norm_gain).astype(jnp.bfloat16)
        gate = jnp.dot(normed, gate_weight, preferred_element_type=jnp.float32)
        up_proj = jnp.dot(normed, up_weight, preferred_element_type=jnp.float32)
        hidden = (jax.nn.silu(gate) * up_proj).astype(jnp.bfloat16)
        mixed = jnp.dot(hidden, down_weight, preferred_element_type=jnp.float32)
        return lax.optimization_barrier(jnp.sum((values + mixed).reshape(CG, STEPS, D), axis=1))
    summed = lax.map(layer_block, states.reshape(TOKENS // group_tokens, group_tokens, D))
    pooled = (summed.reshape(CANDS, D) / STEPS).astype(jnp.bfloat16)
    candidate = unit_rows(jnp.dot(pooled, proj_weight, preferred_element_type=jnp.float32))
    encoded = unit_rows(jnp.dot(private_rows, enc_weight, preferred_element_type=jnp.float32))
    slab = jnp.arange(ROWS, dtype=jnp.int32) // ROW_DEV
    owner = slab * USERS_DEV + user_ids
    counts = jax.ops.segment_sum(jnp.ones((ROWS,), jnp.float32), owner, num_segments=ROWS // 8)
    row_cap = jnp.minimum(1.0, CAP / counts[owner])
    scale = CANDS / ROWS

    def vote_block(index):
        start = (index * ROW_DEV).astype(jnp.int32)
        rows_here = lax.dynamic_slice_in_dim(encoded, start, ROW_DEV, 0)
        cap_here = lax.dynamic_slice_in_dim(row_cap, start, ROW_DEV, 0)
        scores = jnp.dot(rows_here, candidate.T, preferred_element_type=jnp.float32)
        kernel = jnp.exp(scores * 60.0)
        totals = lax.optimization_barrier(jnp.sum(kernel, axis=1))
        weight_rows = cap_here / totals * scale
        return jnp.dot(weight_rows, kernel, precision=lax.Precision.HIGHEST)
    blocks = lax.map(vote_block, jnp.arange(ROWS // ROW_DEV, dtype=jnp.int32))
    votes = lax.optimization_barrier(jnp.sum(blocks, axis=0))
    return votes.reshape(N_USER, N_CAND, CG)
```

```python
import jax
import jax.numpy as jnp
from jax import lax
from jax.experimental import pallas as pl
from jax.experimental.pallas import tpu as pltpu
from jax.sharding import Mesh, PartitionSpec as P

STEPS = 4
CAP = 8
USERS_DEV = 32
CHUNKS = 4
F32 = jnp.float32
BF16 = jnp.bfloat16


def z_index(z):
    return (z % 4) * 2 + z // 4


def shift_z(a, k):
    return lax.ppermute(a, ("zl", "zh"), [(z_index(z), z_index((z + k) % 8)) for z in range(8)])


def swap_core(a):
    return lax.ppermute(a, "core", [(0, 1), (1, 0)])


def shift(a, axis, k):
    return lax.ppermute(a, axis, [(i, (i + k) % 4) for i in range(4)])


def unit_rows(matrix):
    return (matrix * lax.rsqrt(jnp.sum(matrix * matrix, axis=1, keepdims=True) + 1e-06)).astype(BF16)


def pick(a, i, axis=0):
    return lax.dynamic_index_in_dim(a, i, axis, keepdims=False)


def half_weights(gate, up, down, c):
    def cut(w, axis):
        full = lax.dynamic_slice_in_dim(w, c * 512, 384, axis)
        rest = lax.dynamic_slice_in_dim(w, 384 + c * 64, 64, axis)
        return full, rest

    gf, gr = cut(gate, 1)
    uf, ur = cut(up, 1)
    df, dr = cut(down, 0)
    gu = jnp.concatenate([gf, uf, gr, ur], axis=1)
    dn = jnp.concatenate(
        [
            df[0:128],
            df[128:256],
            df[256:384],
            jnp.concatenate([dr[:, :128], dr[:, 128:]], axis=0),
        ],
        axis=1,
    )
    return jnp.concatenate([gu, dn], axis=0)


def relay_states(own, zl):
    up_got, dn_got = [], []
    for t in range(CHUNKS + 3):
        up = own[0, min(t, CHUNKS - 1)]
        dn = own[1, min(t, CHUNKS - 1)]
        if t > 0:
            up = jnp.where(zl == 3, up, up_got[-1])
            dn = jnp.where(zl == 0, dn, dn_got[-1])
        up_got.append(shift_z(up, 1))
        dn_got.append(shift_z(dn, -1))
    up = lax.dynamic_slice_in_dim(jnp.concatenate(up_got, 0), zl * own.shape[2], CHUNKS * own.shape[2], 0)
    dn = lax.dynamic_slice_in_dim(
        jnp.concatenate(dn_got, 0), (3 - zl) * own.shape[2], CHUNKS * own.shape[2], 0
    )
    return up, dn


def ring_z(a):
    h = a.shape[0] // 2
    left = shift_z(a, 1)
    right = shift_z(a, -1)
    far = jnp.concatenate([shift_z(left[:h], 1), shift_z(right[h:], -1)], 0)
    return jnp.stack([a, right, far, left], 0)


def ff_kernel(own_ref, ra_ref, rb_ref, w_ref, hp_ref, acc):
    k = pl.program_id(0)

    @pl.when(k == 0)
    def _():
        acc[...] = jnp.zeros_like(acc)

    w = jnp.concatenate([w_ref[i, 0:256, :] for i in range(4)], axis=0)
    acc[0:512, :] += jnp.dot(own_ref[...], w, preferred_element_type=F32)
    acc[512:768, :] += jnp.dot(ra_ref[...], w, preferred_element_type=F32)
    acc[768:1024, :] += jnp.dot(rb_ref[...], w, preferred_element_type=F32)

    @pl.when(k == 3)
    def _():
        row = lax.broadcasted_iota(jnp.int32, (64, 256), 0)
        col = lax.broadcasted_iota(jnp.int32, (64, 256), 1)
        pool = (col // STEPS == row).astype(BF16)
        lane = lax.broadcasted_iota(jnp.int32, (256, 128), 1)
        for i in range(4):
            rows = pl.ds(i * 256, 256)
            gate = acc[rows, 0:384]
            up = acc[rows, 384:768]
            last = acc[rows, 768:896]
            hidden = (jax.nn.silu(gate) * up).astype(BF16)
            rest = jnp.where(lane < 64, jax.nn.silu(last) * pltpu.roll(last, 64, 1), 0.0).astype(BF16)
            hp_ref[pl.ds(i * 64, 64), 0:384] = jnp.dot(pool, hidden, preferred_element_type=F32).astype(BF16)
            hp_ref[pl.ds(i * 64, 64), 384:512] = jnp.dot(pool, rest, preferred_element_type=F32).astype(BF16)


def feed_forward(own, ra, rb, weights):
    d = own.shape[1]
    return pl.pallas_call(
        ff_kernel,
        out_shape=jax.ShapeDtypeStruct((256, 512), BF16),
        grid=(4,),
        in_specs=[
            pl.BlockSpec((512, d // 4), lambda k: (0, k)),
            pl.BlockSpec((256, d // 4), lambda k: (0, k)),
            pl.BlockSpec((256, d // 4), lambda k: (0, k)),
            pl.BlockSpec((4, 384, 896), lambda k: (k, 0, 0)),
        ],
        out_specs=pl.BlockSpec((256, 512), lambda k: (0, 0)),
        scratch_shapes=[pltpu.VMEM((1024, 896), F32)],
        name="feed_forward",
    )(own, ra, rb, weights)


def w2_kernel(z_ref, d_ref, p_ref, out_ref, acc):
    k = pl.program_id(0)

    @pl.when(k == 0)
    def _():
        acc[...] = jnp.zeros_like(acc)

    for i in range(4):
        p = p_ref[i]
        for j in range(3):
            acc[pl.ds(j * 128, 128), :] += jnp.dot(
                d_ref[i, :, pl.ds(j * 256, 256)], p, preferred_element_type=F32
            )
        acc[384:448, :] += jnp.dot(d_ref[i, 0:64, 768:896], p[0:128], preferred_element_type=F32)
        acc[384:448, :] += jnp.dot(d_ref[i, 64:128, 768:896], p[128:256], preferred_element_type=F32)

    @pl.when(k == 3)
    def _():
        out_ref[...] = acc[...].astype(BF16)


def down_proj(weights, proj_cols, zl):
    return pl.pallas_call(
        w2_kernel,
        out_shape=jax.ShapeDtypeStruct((512, 256), BF16),
        grid_spec=pltpu.PrefetchScalarGridSpec(
            num_scalar_prefetch=1,
            grid=(4,),
            in_specs=[
                pl.BlockSpec((4, 128, 896), lambda k, z: (k, 2, 0)),
                pl.BlockSpec((pl.Squeezed(), 4, 256, 256), lambda k, z: (lax.rem(k - z[0] + 4, 4), 0, 0, 0)),
            ],
            out_specs=pl.BlockSpec((512, 256), lambda k, z: (0, 0)),
            scratch_shapes=[pltpu.VMEM((512, 256), F32)],
        ),
        name="down_proj",
    )(zl.reshape(1), weights, proj_cols)


def shards(states, norm_gain, gate, up, down, proj, rows, enc, ids):
    zl, core, c = lax.axis_index("zl"), lax.axis_index("core"), lax.axis_index("zh")
    y = lax.axis_index("y")
    gen = zl * 2 + core
    pack = half_weights(gate, up, down, c)
    weights = lax.all_gather(pack, ("x", "y"), axis=0)
    values = states.astype(F32)
    normed = (
        values * lax.rsqrt(jnp.mean(values * values, axis=1, keepdims=True) + 1e-05) * norm_gain
    ).astype(BF16)
    mine = pick(normed.reshape(2, 2, CHUNKS, -1, normed.shape[1]), core)
    got_up, got_dn = relay_states(mine, zl)
    part = jnp.concatenate([got_up, got_dn], 0)
    other = swap_core(part)
    encoded = unit_rows(jnp.dot(rows, enc, preferred_element_type=F32))
    cols = lax.dynamic_slice_in_dim(proj, y * 256, 256, 1)
    cols = jnp.concatenate([cols[i * 128 : (i + 1) * 128] for i in range(4)], axis=1)
    bundle = ring_z(jnp.concatenate([encoded, cols], 0))
    bundle2 = swap_core(bundle)
    both = jnp.stack([bundle, bundle2], 1)
    all_rows = both[:, :, :256]
    first = jnp.where(core == 0, bundle[:, 256:], bundle2[:, 256:])
    second = jnp.where(core == 0, bundle2[:, 256:], bundle[:, 256:])
    proj_cols = jnp.stack([first, second], 1)
    proj_cols = jnp.concatenate([proj_cols[..., i * 256 : (i + 1) * 256] for i in range(4)], axis=2)
    proj_cols = proj_cols.reshape(4, 4, 256, 256)
    pool = (jnp.arange(512)[None, :] // STEPS == jnp.arange(128)[:, None]).astype(BF16)
    state_cols = lax.dynamic_slice_in_dim(states, gen * 512, 512, 1)
    resid = jnp.dot(pool, state_cols, preferred_element_type=F32).astype(BF16)
    resid = jnp.dot(resid, proj, preferred_element_type=F32)
    w2_cols = down_proj(weights, proj_cols, zl)
    w2_parts = jnp.stack([w2_cols, shift(w2_cols, "y", -1), shift(w2_cols, "y", 2), shift(w2_cols, "y", 1)], 0)
    hp = feed_forward(normed, part, other, weights)
    hp_own, hp_a, hp_b = hp[:128], hp[128:192], hp[192:]
    hp_other = jnp.where(core == 0, jnp.concatenate([hp_a, hp_b], 0), jnp.concatenate([hp_b, hp_a], 0))
    hp_all = jnp.where(
        c == 0, jnp.concatenate([hp_own, hp_other], 0), jnp.concatenate([hp_other, hp_own], 0)
    )
    w2 = jnp.concatenate([pick(w2_parts, (i - y) % 4) for i in range(4)], axis=1)
    emb = jnp.dot(hp_all, w2, preferred_element_type=F32).reshape(2, 128, -1)
    emb = jnp.concatenate(
        [(emb[i] + jnp.where(c == i, resid, 0.0))[None] for i in range(2)], 0
    ) * (1.0 / STEPS)
    emb = emb.reshape(2, 4, 2, 16, -1)
    keep = pick(emb, core, 2)
    send = pick(emb, 1 - core, 2)
    emb = (keep + swap_core(send)).astype(BF16)
    emb = lax.all_to_all(emb.transpose(1, 0, 2, 3).reshape(8, 16, -1), ("zl", "zh"), 0, 0)
    candidate = unit_rows(jnp.sum(emb.astype(F32), axis=0))
    cands = lax.all_to_all(
        jnp.broadcast_to(candidate[None], (16,) + candidate.shape), ("x", "y"), 0, 0
    ).reshape(256, -1)
    scores = lax.dot_general(
        cands, all_rows.reshape(2048, -1), (((1,), (1,)), ((), ())), preferred_element_type=F32
    )
    kernel = jnp.exp(scores * 60.0)
    totals = jnp.sum(kernel, axis=0).reshape(4, 2, 256)
    totals = jnp.roll(jnp.roll(totals, zl, 0), core, 1)
    member = (ids[:, None] == jnp.arange(USERS_DEV, dtype=jnp.int32)[None, :]).astype(F32)
    counts = jnp.sum(member, axis=0)
    limit = jnp.minimum(1.0, CAP / jnp.maximum(counts, 1.0))
    row_cap = jnp.dot(member, limit, precision=lax.Precision.HIGHEST)
    note = jnp.concatenate([totals.reshape(16, 128), row_cap.reshape(2, 128)], 0)
    notes = lax.all_to_all(jnp.broadcast_to(note[None], (16, 18, 128)), ("zl", "core", "zh"), 0, 0)
    totals = jnp.sum(notes[:, :16], axis=0).reshape(4, 2, 256)
    caps = notes[:, 16:].reshape(4, 2, 2, 256)[:, :, 0]
    weight = caps / totals * (4096 / 32768)
    weight = jnp.roll(jnp.roll(weight, -zl, 0), -core, 1)
    partial = jnp.sum(kernel * weight.reshape(1, 2048), axis=1)
    partial = lax.all_to_all(
        jnp.broadcast_to(partial.reshape(1, 2, 128), (128, 2, 128)), ("zl", "core", "x", "y"), 0, 0
    )
    votes = jnp.sum(partial.reshape(8, 16, 16, 16), axis=1)
    return votes.transpose(1, 0, 2).reshape(16, 1, 128)


def solution(mesh):
    fine = Mesh(mesh.devices.reshape(4, 2, 4, 4, 2), ("zl", "core", "x", "y", "zh"))
    gen, user, cand = ("zl", "core"), ("x", "y"), "zh"
    return jax.shard_map(
        shards,
        mesh=fine,
        in_specs=(
            P(user + (cand,), None),
            P(),
            P(user, gen),
            P(user, gen),
            P(gen, user),
            P(gen, None),
            P(gen + user, None),
            P(),
            P(gen + user),
        ),
        out_specs=P(None, cand, None),
        check_vma=False,
    )
```

```python
import functools

import jax
import jax.numpy as jnp
from jax import lax
from jax.experimental import pallas as pl
from jax.experimental.pallas import tpu as pltpu
from jax.sharding import Mesh, PartitionSpec as P

STEPS = 4
CAP = 8
F32 = jnp.float32
BF16 = jnp.bfloat16
SMEM = pl.BlockSpec(memory_space=pltpu.SMEM)
ANY = pl.BlockSpec(memory_space=pl.ANY)
VMEM = pl.BlockSpec(memory_space=pltpu.VMEM)
X, Y, ZL, CORE, ZH, PLACES = 0, 1, 2, 3, 4, 5


def z_pairs(pairs):
    place = lambda z: (z % 4) * 2 + z // 4
    return [(place(a % 8), place(b % 8)) for a, b in pairs]


def shift_z(a, k):
    return lax.ppermute(a, ("zl", "zh"), z_pairs([(z, z + k) for z in range(8)]))


def send_z(a, pairs):
    return lax.ppermute(a, ("zl", "zh"), z_pairs(pairs))


def shift(a, axis, k):
    return lax.ppermute(a, axis, [(i, (i + k) % 4) for i in range(4)])


def swap_core(a):
    return lax.ppermute(a, "core", [(0, 1), (1, 0)])


def pick(a, i, axis=0):
    return lax.dynamic_index_in_dim(a, i, axis, keepdims=False)


def half_weights(gate, up, down, c):
    def cut(w, axis):
        full = lax.dynamic_slice_in_dim(w, c * 512, 384, axis)
        rest = lax.dynamic_slice_in_dim(w, 384 + c * 64, 64, axis)
        return full, rest

    gf, gr = cut(gate, 1)
    uf, ur = cut(up, 1)
    gu = jnp.concatenate([gf, uf, gr, ur], axis=1)
    dn = jnp.concatenate(cut(down, 0), axis=0)
    chunks = []
    for i in range(2):
        cols = dn[:, i * 128 : (i + 1) * 128]
        flat = jnp.concatenate([cols[j * 64 : (j + 1) * 64] for j in range(7)], axis=1)
        chunks.append(jnp.concatenate([gu[i * 128 : (i + 1) * 128], flat], axis=0))
    return chunks


def gather_colour(chunk, first, second):
    near = jnp.stack([chunk, shift(chunk, first, -1), shift(chunk, first, 2), shift(chunk, first, 1)], 0)
    plus = shift(near, second, -1)
    minus = shift(near, second, 1)
    far_lo = shift(minus[:2], second, 1)
    far_hi = shift(plus[2:], second, -1)
    return near, plus, minus, far_lo, far_hi


def exchange_states(mine, zl):
    q = send_z(pick(mine, 3 - zl), [(z, 7 - z) for z in range(8)])
    first, last = zl == 0, zl == 3
    p1 = shift_z(jnp.where(last, mine[2], q), 1)
    p2 = shift_z(jnp.where(first, mine[1], q), -1)
    p3 = send_z(jnp.where(last, mine[3], q), [(0, 2), (4, 6), (3, 4), (7, 0)])
    p4 = send_z(jnp.where(first, mine[0], q), [(3, 1), (7, 5), (0, 7), (4, 3)])
    return jnp.concatenate([q, p1, p2, p3 + p4], 0)


def user_of(info, colour, m, k):
    x, y = info[X], info[Y]
    if colour == 0:
        return lax.rem(x + k, 4), lax.rem(y + m, 4)
    return lax.rem(x + m, 4), lax.rem(y + k, 4)


def ff_kernel(spec, last, info, own, part, other, *refs):
    n = len(spec)
    bundles, refs = refs[:n], refs[n:]
    if last:
        acc_in, hp_ref, tok, acc, sems = refs[0], refs[1], refs[2], refs[3], refs[4]
        held = refs[5:]
    else:
        acc, tok, sems = refs[0], refs[1], refs[2]
        held = refs[3:]
    copies = [pltpu.make_async_copy(b, h, sems.at[i]) for i, (b, h) in enumerate(zip(bundles, held))]
    toks = [
        pltpu.make_async_copy(own, tok.at[pl.ds(0, 512)], sems.at[n]),
        pltpu.make_async_copy(part, tok.at[pl.ds(512, 256)], sems.at[n + 1]),
        pltpu.make_async_copy(other, tok.at[pl.ds(768, 256)], sems.at[n + 2]),
    ]
    copies[0].start()
    toks[0].start()
    for copy in copies[1:]:
        copy.start()
    if last:
        old = pltpu.make_async_copy(acc_in, acc, sems.at[n + 3])
        old.start()
    toks[1].start()
    toks[2].start()
    toks[0].wait()
    if last:
        old.wait()
    for i in range(2):
        rows = pl.ds(i * 512, 512)
        if i == 1:
            toks[1].wait()
            toks[2].wait()
        for b, (colour, m, k0, nk) in enumerate(spec):
            if i == 0:
                copies[b].wait()
            xs, ws = [], []
            for k in range(nk):
                ux, uy = user_of(info, colour, m, k0 + k)
                col = pl.multiple_of((ux * 4 + uy) * 256 + colour * 128, 128)
                xs.append(tok[rows, pl.ds(col, 128)])
                ws.append(held[b][k, 0:128, :])
            d = jnp.dot(jnp.concatenate(xs, 1), jnp.concatenate(ws, 0), preferred_element_type=F32)
            if b == 0 and not last:
                acc[rows, :] = d
            else:
                acc[rows, :] += d
        if last:
            row = lax.broadcasted_iota(jnp.int32, (64, 256), 0)
            col = lax.broadcasted_iota(jnp.int32, (64, 256), 1)
            pool = (col // STEPS == row).astype(BF16)
            lane = lax.broadcasted_iota(jnp.int32, (256, 128), 1)
            for j in range(2 * i, 2 * i + 2):
                at = pl.ds(j * 256, 256)
                gate = acc[at, 0:384]
                up = acc[at, 384:768]
                mixed = acc[at, 768:896]
                hidden = (jax.nn.silu(gate) * up).astype(BF16)
                rest = jnp.where(lane < 64, jax.nn.silu(mixed) * pltpu.roll(mixed, 64, 1), 0.0).astype(BF16)
                hp = jnp.dot(pool, hidden, preferred_element_type=F32).astype(BF16)
                hp_rest = jnp.dot(pool, rest, preferred_element_type=F32).astype(BF16)
                for t in range(4):
                    place = pl.ds(pl.multiple_of(info[PLACES + j * 4 + t] * 16, 16), 16)
                    hp_ref[place, 0:384] = hp[t * 16 : (t + 1) * 16]
                    hp_ref[place, 384:512] = hp_rest[t * 16 : (t + 1) * 16]


def feed_forward(spec, info, own, part, other, bundles, acc=None):
    last = acc is not None
    scratch = [pltpu.VMEM((1024, 4096), BF16)]
    if last:
        scratch.append(pltpu.VMEM((1024, 896), F32))
    scratch.append(pltpu.SemaphoreType.DMA((len(spec) + 4,)))
    scratch += [pltpu.VMEM(b.shape, BF16) for b in bundles]
    out = jax.ShapeDtypeStruct((256, 512), BF16) if last else jax.ShapeDtypeStruct((1024, 896), F32)
    args = (info, own, part, other, *bundles) + ((acc,) if last else ())
    return pl.pallas_call(
        functools.partial(ff_kernel, spec, last),
        out_shape=out,
        in_specs=[SMEM] + [ANY] * (len(args) - 1),
        out_specs=VMEM,
        scratch_shapes=scratch,
        name="feed_forward_last" if last else "feed_forward_first",
    )(*args)


def w2_kernel(spec, last, info, mine, theirs, *refs):
    n = len(spec)
    bundles, refs = refs[:n], refs[n:]
    acc = refs[0][...] if last else None
    out = refs[1] if last else refs[0]
    for b, (colour, m, k0, nk) in enumerate(spec):
        ds, ps = [], []
        for k in range(nk):
            ux, uy = user_of(info, colour, m, k0 + k)
            flat = bundles[b][k, 128:192, :]
            ds.append(jnp.concatenate([flat[:, j * 128 : (j + 1) * 128] for j in range(7)], 0))
            rel = lax.rem(ux - info[ZL] + 4, 4)
            col = pl.ds(pl.multiple_of((lax.rem(uy, 2) * 2 + colour) * 256, 256), 256)
            same = uy // 2 == info[CORE]
            ps.append(jnp.where(same, mine[rel, :, col], theirs[rel, :, col]))
        d = jnp.dot(jnp.concatenate(ds, 1), jnp.concatenate(ps, 0), preferred_element_type=F32)
        acc = d if acc is None else acc + d
    if last:
        out[0:448, :] = acc.astype(BF16)
        out[448:512, :] = jnp.zeros((64, 256), BF16)
    else:
        out[...] = acc


def down_proj(spec, info, mine, theirs, bundles, acc=None):
    last = acc is not None
    args = (info, mine, theirs, *bundles) + ((acc,) if last else ())
    out = jax.ShapeDtypeStruct((512, 256), BF16) if last else jax.ShapeDtypeStruct((448, 256), F32)
    return pl.pallas_call(
        functools.partial(w2_kernel, spec, last),
        out_shape=out,
        in_specs=[SMEM] + [VMEM] * (len(args) - 1),
        out_specs=VMEM,
        name="down_proj_last" if last else "down_proj_first",
    )(*args)


def embed_kernel(info, hp, w0, w1, w2, w3, resid, keep, send, emb):
    for k, w in enumerate((w0, w1, w2, w3)):
        col = pl.ds(pl.multiple_of(lax.rem(info[Y] + k, 4) * 256, 256), 256)
        emb[:, col] = jnp.dot(hp[...], w[...], preferred_element_type=F32)
    half = pl.ds(pl.multiple_of(info[ZH] * 128, 128), 128)
    emb[half, :] += resid[...]
    for z in range(4):
        for c in range(2):
            at = pl.ds((z * 2 + c) * 16, 16)
            base = c * 128 + z * 32
            keep[at, :] = emb[pl.ds(pl.multiple_of(base + info[CORE] * 16, 16), 16), :] * (1.0 / STEPS)
            send[at, :] = emb[pl.ds(pl.multiple_of(base + 16 - info[CORE] * 16, 16), 16), :] * (1.0 / STEPS)


def embed(info, hp, parts, resid):
    shape = jax.ShapeDtypeStruct((128, 1024), F32)
    return pl.pallas_call(
        embed_kernel,
        out_shape=(shape, shape),
        in_specs=[SMEM] + [VMEM] * 6,
        out_specs=(VMEM, VMEM),
        scratch_shapes=[pltpu.VMEM((256, 1024), F32)],
        name="embed",
    )(info, hp, *parts, resid)


def unit_rows(matrix):
    return (matrix * lax.rsqrt(jnp.sum(matrix * matrix, axis=1, keepdims=True) + 1e-06)).astype(BF16)


def candidate_kernel(parts, out):
    total = parts[0].astype(F32)
    for i in range(1, 8):
        total += parts[i].astype(F32)
    cand = unit_rows(total)
    for i in range(16):
        out[i] = cand


def candidates(parts):
    return pl.pallas_call(
        candidate_kernel,
        out_shape=jax.ShapeDtypeStruct((16, 16, 1024), BF16),
        in_specs=[VMEM],
        out_specs=VMEM,
        name="candidates",
    )(parts)


def row_of(info, b):
    k, s = b % 4, b // 4
    core = info[CORE] if s == 0 else 1 - info[CORE]
    return core * 4 + lax.rem(info[X] + k, 4)


def score_kernel(info, cands, mine, theirs, ids_row, ids_col, kernel_ref, note_ref, note):
    match = (ids_row[...] == ids_col[...]).astype(F32)
    count = jnp.sum(match, axis=0, keepdims=True)
    note[8:16, :] = jnp.broadcast_to(jnp.minimum(1.0, CAP / count), (8, 256))
    for b in range(8):
        rows = (mine if b < 4 else theirs)[b % 4]
        scores = lax.dot_general(
            cands[...], rows, (((1,), (1,)), ((), ())), preferred_element_type=F32
        )
        kernel = jnp.exp(scores * 60.0)
        kernel_ref[:, b * 256 : (b + 1) * 256] = kernel
        note[pl.ds(row_of(info, b), 1), :] = jnp.sum(kernel, axis=0, keepdims=True)
    for i in range(16):
        note_ref[i] = note[...]


def score(info, cands, mine, theirs, ids):
    return pl.pallas_call(
        score_kernel,
        out_shape=(
            jax.ShapeDtypeStruct((256, 2048), F32),
            jax.ShapeDtypeStruct((16, 16, 256), F32),
        ),
        in_specs=[SMEM] + [VMEM] * 5,
        out_specs=(VMEM, VMEM),
        scratch_shapes=[pltpu.VMEM((16, 256), F32)],
        name="score",
    )(info, cands, mine, theirs, ids.reshape(1, 256), ids.reshape(256, 1))


def vote_kernel(info, notes, kernel, out, weight):
    totals = notes[0, 0:8, :]
    for i in range(1, 16):
        totals += notes[i, 0:8, :]
    for r in range(8):
        weight[r : r + 1, :] = notes[2 * r, 8:9, :] / totals[r : r + 1] * (4096 / 32768)
    acc = None
    for b in range(8):
        w = weight[pl.ds(row_of(info, b), 1), :]
        part = kernel[:, b * 256 : (b + 1) * 256] * w
        acc = part if acc is None else acc + part
    votes = jnp.sum(acc.T, axis=0, keepdims=True)
    out[...] = jnp.broadcast_to(votes, (128, 256))


def vote(info, notes, kernel):
    return pl.pallas_call(
        vote_kernel,
        out_shape=jax.ShapeDtypeStruct((128, 256), F32),
        in_specs=[SMEM, VMEM, VMEM],
        out_specs=VMEM,
        scratch_shapes=[pltpu.VMEM((8, 256), F32)],
        name="vote",
    )(info, notes, kernel)


def positions(zl, core, x, y, c):
    order = jnp.array([[0, 2, 1, 3], [1, 0, 2, 3], [2, 1, 3, 0], [3, 2, 1, 0]], jnp.int32)
    pieces = pick(order, zl)
    own = c * 8 + jnp.arange(8, dtype=jnp.int32)
    part = (1 - c) * 8 + pieces * 2 + core
    other = (1 - c) * 8 + pieces * 2 + 1 - core
    here = jnp.stack([x, y, zl, core, c]).astype(jnp.int32)
    return jnp.concatenate([here, own, part, other])


NEAR = tuple((colour, m, 0, 4) for colour in range(2) for m in (0, 1, 3))
FAR = tuple((colour, 2, k, 2) for colour in range(2) for k in (0, 2))


def shards(states, norm_gain, gate, up, down, proj, rows, enc, ids):
    zl, core, x, y, c = (lax.axis_index(a) for a in ("zl", "core", "x", "y", "zh"))
    info = positions(zl, core, x, y, c)
    chunk_a, chunk_b = half_weights(gate, up, down, c)
    a0, a1, a3, a2lo, a2hi = gather_colour(chunk_a, "x", "y")
    b0, b1, b3, b2lo, b2hi = gather_colour(chunk_b, "y", "x")
    near = (a0, a1, a3, b0, b1, b3)
    far = (a2lo, a2hi, b2lo, b2hi)
    values = states.astype(F32)
    normed = (
        values * lax.rsqrt(jnp.mean(values * values, axis=1, keepdims=True) + 1e-05) * norm_gain
    ).astype(BF16)
    part = exchange_states(pick(normed.reshape(4, 2, 64, -1), core, 1), zl)
    other = swap_core(part)
    cols = lax.dynamic_slice_in_dim(proj, y * 256, 256, 1)
    cols = jnp.concatenate([cols[i * 128 : (i + 1) * 128] for i in range(4)], axis=1)
    cols = jnp.stack([cols, shift_z(cols, -1), shift_z(cols, 2), shift_z(cols, 1)], 0)
    cols_other = swap_core(cols)
    encoded = unit_rows(jnp.dot(rows, enc, preferred_element_type=F32))
    left, right = shift(encoded, "x", 1), shift(encoded, "x", -1)
    across = jnp.concatenate([shift(left[:128], "x", 1), shift(right[128:], "x", -1)], 0)
    encoded = jnp.stack([encoded, right, across, left], 0)
    encoded_other = swap_core(encoded)
    pool = (jnp.arange(512)[None, :] // STEPS == jnp.arange(128)[:, None]).astype(BF16)
    state_cols = lax.dynamic_slice_in_dim(states, (zl * 2 + core) * 512, 512, 1)
    resid = jnp.dot(pool, state_cols, preferred_element_type=F32).astype(BF16)
    resid = jnp.dot(resid, proj, preferred_element_type=F32)
    acc = feed_forward(NEAR, info, normed, part, other, near)
    w2 = down_proj(NEAR, info, cols, cols_other, near)
    w2 = down_proj(FAR, info, cols, cols_other, far, w2)
    w2 = (w2, shift(w2, "y", -1), shift(w2, "y", 2), shift(w2, "y", 1))
    hp = feed_forward(FAR, info, normed, part, other, far, acc)
    keep, send = embed(info, hp, w2, resid)
    emb = (keep + swap_core(send)).astype(BF16).reshape(8, 16, 1024)
    emb = lax.all_to_all(emb, ("zl", "zh"), 0, 0)
    cands = lax.all_to_all(candidates(emb), ("zl", "y"), 0, 0).reshape(256, 1024)
    kernel, note = score(info, cands, encoded, encoded_other, ids)
    notes = lax.all_to_all(note, ("core", "x", "zh"), 0, 0)
    partial = vote(info, notes, kernel)
    partial = lax.all_to_all(partial.reshape(128, 2, 128), ("zl", "core", "x", "y"), 0, 0)
    votes = jnp.sum(partial.reshape(4, 2, 4, 4, 4, 4, 16), axis=(0, 3))
    return votes.transpose(1, 3, 2, 0, 4).reshape(16, 1, 128)


def solution(mesh):
    fine = Mesh(mesh.devices.reshape(4, 2, 4, 4, 2), ("zl", "core", "x", "y", "zh"))
    gen, user, cand = ("zl", "core"), ("x", "y"), "zh"
    return jax.shard_map(
        shards,
        mesh=fine,
        in_specs=(
            P(user + (cand,), None),
            P(),
            P(user, gen),
            P(user, gen),
            P(gen, user),
            P(gen, None),
            P(gen + user, None),
            P(),
            P(gen + user),
        ),
        out_specs=P(None, cand, None),
        check_vma=False,
    )
```

```python
import functools

import jax
import jax.numpy as jnp
from jax import lax
from jax.experimental import pallas as pl
from jax.experimental.pallas import tpu as pltpu
from jax.sharding import Mesh, PartitionSpec as P

STEPS = 4
CAP = 8
F32 = jnp.float32
BF16 = jnp.bfloat16
VMEM = pl.BlockSpec(memory_space=pltpu.VMEM)


def z_pairs(pairs):
    place = lambda z: (z % 4) * 2 + z // 4
    return [(place(a % 8), place(b % 8)) for a, b in pairs]


def shift_z(a, k):
    return lax.ppermute(a, ("zl", "zh"), z_pairs([(z, z + k) for z in range(8)]))


def send_z(a, pairs):
    return lax.ppermute(a, ("zl", "zh"), z_pairs(pairs))


def shift(a, axis, k):
    return lax.ppermute(a, axis, [(i, (i + k) % 4) for i in range(4)])


def swap_core(a):
    return lax.ppermute(a, "core", [(0, 1), (1, 0)])


def pick(a, i, axis=0):
    return lax.dynamic_index_in_dim(a, i, axis, keepdims=False)


def pack_kernel(gate, up, down, out):
    c = lax.axis_index("zh")
    full = pl.ds(pl.multiple_of(c * 512, 128), 384)
    out[0:256, 0:384] = gate[:, full]
    out[0:256, 384:768] = up[:, full]
    g = gate[:, 384:512].astype(F32)
    u = up[:, 384:512].astype(F32)
    g = jnp.where(c == 0, g, pltpu.roll(g, 64, 1))
    u = jnp.where(c == 0, pltpu.roll(u, 64, 1), u)
    lane = lax.broadcasted_iota(jnp.int32, (256, 128), 1)
    out[0:256, 768:896] = jnp.where(lane < 64, g, u).astype(BF16)
    for i in range(2):
        for j in range(7):
            start = 384 + c * 64 if j == 6 else c * 512 + j * 64
            rows = pl.ds(pl.multiple_of(start, 64), 64)
            out[256 + i * 64 : 320 + i * 64, j * 128 : (j + 1) * 128] = down[rows, i * 128 : (i + 1) * 128]


def pack_weights(gate, up, down):
    return pl.pallas_call(
        pack_kernel,
        out_shape=jax.ShapeDtypeStruct((384, 896), BF16),
        in_specs=[VMEM] * 3,
        out_specs=VMEM,
        name="pack_weights",
    )(gate, up, down)


def norm_kernel(states, gain, normed, mine, piece):
    zl, core = lax.axis_index("zl"), lax.axis_index("core")
    values = states[...].astype(F32)
    scale = lax.rsqrt(jnp.mean(values * values, axis=1, keepdims=True) + 1e-05)
    normed[...] = (values * scale * gain[...]).astype(BF16)
    part = normed[pl.ds(pl.multiple_of(core * 64, 64), 64), :]
    mine[0] = part

    @pl.when(pl.program_id(0) == 3 - zl)
    def _():
        piece[...] = part


def norm(states, gain):
    d = states.shape[1]
    return pl.pallas_call(
        norm_kernel,
        out_shape=(
            jax.ShapeDtypeStruct((512, d), BF16),
            jax.ShapeDtypeStruct((4, 64, d), BF16),
            jax.ShapeDtypeStruct((64, d), BF16),
        ),
        grid=(4,),
        in_specs=[
            pl.BlockSpec((128, d), lambda i: (i, 0)),
            pl.BlockSpec((1, d), lambda i: (0, 0)),
        ],
        out_specs=(
            pl.BlockSpec((128, d), lambda i: (i, 0)),
            pl.BlockSpec((1, 64, d), lambda i: (i, 0, 0)),
            pl.BlockSpec((64, d), lambda i: (0, 0)),
        ),
        name="norm",
    )(states, gain.reshape(1, d))


def exchange_states(mine, piece, zl):
    q = send_z(piece, [(z, 7 - z) for z in range(8)])
    first, last = zl == 0, zl == 3
    p1 = shift_z(jnp.where(last, mine[2], q), 1)
    p2 = shift_z(jnp.where(first, mine[1], q), -1)
    p3 = send_z(jnp.where(last, mine[3], q), [(0, 2), (4, 6), (3, 4), (7, 0)])
    p4 = send_z(jnp.where(first, mine[0], q), [(3, 1), (7, 5), (0, 7), (4, 3)])
    return jnp.concatenate([q, p1, p2, p3 + p4], 0)


def places():
    zl, core, c = lax.axis_index("zl"), lax.axis_index("core"), lax.axis_index("zh")
    pieces = (
        zl,
        jnp.where(zl == 0, 2, zl - 1),
        jnp.where(zl == 3, 1, zl + 1),
        jnp.where(zl < 2, 3, 0),
    )
    own = [c * 8 + i for i in range(8)]
    part = [(1 - c) * 8 + p * 2 + core for p in pieces]
    other = [(1 - c) * 8 + p * 2 + 1 - core for p in pieces]
    return own + part + other


def ff_kernel(own, part, other, w_ref, hp_ref, acc):
    k = pl.program_id(0)
    w = jnp.concatenate([w_ref[i] for i in range(4)], axis=0)
    pairs = ((pl.ds(0, 512), own), (pl.ds(512, 256), part), (pl.ds(768, 256), other))

    @pl.when(k == 0)
    def _():
        for rows, tokens in pairs:
            acc[rows, :] = jnp.dot(tokens[...], w, preferred_element_type=F32)

    @pl.when(k > 0)
    def _():
        for rows, tokens in pairs:
            acc[rows, :] += jnp.dot(tokens[...], w, preferred_element_type=F32)

    @pl.when(k == 3)
    def _():
        row = lax.broadcasted_iota(jnp.int32, (64, 256), 0)
        col = lax.broadcasted_iota(jnp.int32, (64, 256), 1)
        pool = (col // STEPS == row).astype(BF16)
        lane = lax.broadcasted_iota(jnp.int32, (256, 128), 1)
        place = places()
        for j in range(4):
            at = pl.ds(j * 256, 256)
            gate = acc[at, 0:384]
            up = acc[at, 384:768]
            mixed = acc[at, 768:896]
            hidden = (jax.nn.silu(gate) * up).astype(BF16)
            rest = jnp.where(lane < 64, jax.nn.silu(mixed) * pltpu.roll(mixed, 64, 1), 0.0).astype(BF16)
            hp = jnp.dot(pool, hidden, preferred_element_type=F32).astype(BF16)
            hp_rest = jnp.dot(pool, rest, preferred_element_type=F32).astype(BF16)
            for t in range(4):
                to = pl.ds(pl.multiple_of(place[j * 4 + t] * 16, 16), 16)
                hp_ref[to, 0:384] = hp[t * 16 : (t + 1) * 16]
                hp_ref[to, 384:512] = hp_rest[t * 16 : (t + 1) * 16]


def feed_forward(own, part, other, weights):
    return pl.pallas_call(
        ff_kernel,
        out_shape=jax.ShapeDtypeStruct((256, 512), BF16),
        grid=(4,),
        in_specs=[
            pl.BlockSpec((512, 1024), lambda k: (0, k)),
            pl.BlockSpec((256, 1024), lambda k: (0, k)),
            pl.BlockSpec((256, 1024), lambda k: (0, k)),
            pl.BlockSpec((4, 256, 896), lambda k: (k, 0, 0)),
        ],
        out_specs=pl.BlockSpec((256, 512), lambda k: (0, 0)),
        scratch_shapes=[pltpu.VMEM((1024, 896), F32)],
        name="feed_forward",
    )(own, part, other, weights)


def w2_kernel(d_ref, mine, theirs, out, acc):
    x = pl.program_id(0)
    zl, core = lax.axis_index("zl"), lax.axis_index("core")
    rel = lax.rem(x - zl + 4, 4)
    ds, ps = [], []
    for y in range(4):
        for i in range(2):
            tiles = [d_ref[y, i * 64 : (i + 1) * 64, j * 128 : (j + 1) * 128] for j in range(7)]
            ds.append(jnp.concatenate(tiles, 0))
            col = slice(((y % 2) * 2 + i) * 256, ((y % 2) * 2 + i + 1) * 256)
            ps.append(jnp.where(core == y // 2, mine[rel, :, col], theirs[rel, :, col]))
    d = jnp.dot(jnp.concatenate(ds, 1), jnp.concatenate(ps, 0), preferred_element_type=F32)

    @pl.when(x == 0)
    def _():
        acc[...] = d

    @pl.when(x > 0)
    def _():
        acc[...] += d

    @pl.when(x == 3)
    def _():
        out[0:448, :] = acc[...].astype(BF16)
        out[448:512, :] = jnp.zeros((64, 256), BF16)


def down_proj(weights, mine, theirs):
    whole = pl.BlockSpec((4, 128, 1024), lambda k: (0, 0, 0))
    return pl.pallas_call(
        w2_kernel,
        out_shape=jax.ShapeDtypeStruct((512, 256), BF16),
        grid=(4,),
        in_specs=[pl.BlockSpec((4, 128, 896), lambda k: (k, 2, 0)), whole, whole],
        out_specs=pl.BlockSpec((512, 256), lambda k: (0, 0)),
        scratch_shapes=[pltpu.VMEM((448, 256), F32)],
        name="down_proj",
    )(weights, mine, theirs)


def embed_kernel(hp, w0, w1, w2, w3, resid, keep, send, emb):
    y, core, zh = lax.axis_index("y"), lax.axis_index("core"), lax.axis_index("zh")
    for k, w in enumerate((w0, w1, w2, w3)):
        col = pl.ds(pl.multiple_of(lax.rem(y + k, 4) * 256, 256), 256)
        emb[:, col] = jnp.dot(hp[...], w[...], preferred_element_type=F32)
    half = pl.ds(pl.multiple_of(zh * 128, 128), 128)
    emb[half, :] += resid[...]
    for z in range(4):
        for c in range(2):
            at = pl.ds((z * 2 + c) * 16, 16)
            base = c * 128 + z * 32
            keep[at, :] = emb[pl.ds(pl.multiple_of(base + core * 16, 16), 16), :] * (1.0 / STEPS)
            send[at, :] = emb[pl.ds(pl.multiple_of(base + 16 - core * 16, 16), 16), :] * (1.0 / STEPS)


def embed(hp, parts, resid):
    shape = jax.ShapeDtypeStruct((128, 1024), F32)
    return pl.pallas_call(
        embed_kernel,
        out_shape=(shape, shape),
        in_specs=[VMEM] * 6,
        out_specs=(VMEM, VMEM),
        scratch_shapes=[pltpu.VMEM((256, 1024), F32)],
        name="embed",
    )(hp, *parts, resid)


def unit_rows(matrix):
    return (matrix * lax.rsqrt(jnp.sum(matrix * matrix, axis=1, keepdims=True) + 1e-06)).astype(BF16)


def candidate_kernel(parts, out):
    total = parts[0].astype(F32)
    for i in range(1, 8):
        total += parts[i].astype(F32)
    cand = unit_rows(total)
    for i in range(16):
        out[i] = cand


def candidates(parts):
    return pl.pallas_call(
        candidate_kernel,
        out_shape=jax.ShapeDtypeStruct((16, 16, 1024), BF16),
        in_specs=[VMEM],
        out_specs=VMEM,
        name="candidates",
    )(parts)


def row_of(b):
    k, s = b % 4, b // 4
    core = lax.axis_index("core")
    core = core if s == 0 else 1 - core
    return lax.rem(lax.axis_index("zl") + k, 4) * 2 + core


def score_kernel(cands, mine, theirs, ids_row, ids_col, kernel_ref, note_ref, note):
    match = (ids_row[...] == ids_col[...]).astype(F32)
    count = jnp.sum(match, axis=0, keepdims=True)
    note[8:16, :] = jnp.broadcast_to(jnp.minimum(1.0, CAP / count), (8, 256))
    for b in range(8):
        rows = (mine if b < 4 else theirs)[b % 4]
        scores = lax.dot_general(
            cands[...], rows, (((1,), (1,)), ((), ())), preferred_element_type=F32
        )
        kernel = jnp.exp(scores * 60.0)
        kernel_ref[:, b * 256 : (b + 1) * 256] = kernel
        note[pl.ds(row_of(b), 1), :] = jnp.sum(kernel, axis=0, keepdims=True)
    for i in range(16):
        note_ref[i] = note[...]


def score(cands, mine, theirs, ids):
    return pl.pallas_call(
        score_kernel,
        out_shape=(
            jax.ShapeDtypeStruct((256, 2048), F32),
            jax.ShapeDtypeStruct((16, 16, 256), F32),
        ),
        in_specs=[VMEM] * 5,
        out_specs=(VMEM, VMEM),
        scratch_shapes=[pltpu.VMEM((16, 256), F32)],
        name="score",
    )(cands, mine, theirs, ids.reshape(1, 256), ids.reshape(256, 1))


def vote_kernel(notes, kernel, out, weight):
    totals = notes[0, 0:8, :]
    for i in range(1, 16):
        totals += notes[i, 0:8, :]
    for r in range(8):
        weight[r : r + 1, :] = notes[2 * r, 8:9, :] / totals[r : r + 1] * (4096 / 32768)
    acc = None
    for b in range(8):
        w = weight[pl.ds(row_of(b), 1), :]
        part = kernel[:, b * 256 : (b + 1) * 256] * w
        acc = part if acc is None else acc + part
    votes = jnp.sum(acc.T, axis=0, keepdims=True)
    pair = jnp.concatenate([votes[:, :128], votes[:, 128:]], 0)
    out[...] = jnp.broadcast_to(pair[None], (128, 2, 128))


def vote(notes, kernel):
    return pl.pallas_call(
        vote_kernel,
        out_shape=jax.ShapeDtypeStruct((128, 2, 128), F32),
        in_specs=[VMEM, VMEM],
        out_specs=VMEM,
        scratch_shapes=[pltpu.VMEM((8, 256), F32)],
        name="vote",
    )(notes, kernel)


def shards(states, norm_gain, gate, up, down, proj, rows, enc, ids):
    zl, core, y = lax.axis_index("zl"), lax.axis_index("core"), lax.axis_index("y")
    weights = lax.all_gather(pack_weights(gate, up, down), ("x", "y"), axis=0)
    normed, mine, piece = norm(states, norm_gain)
    part = exchange_states(mine, piece, zl)
    other = swap_core(part)
    cols = lax.dynamic_slice_in_dim(proj, y * 256, 256, 1)
    cols = jnp.concatenate([cols[i * 128 : (i + 1) * 128] for i in range(4)], axis=1)
    cols = jnp.stack([cols, shift_z(cols, -1), shift_z(cols, 2), shift_z(cols, 1)], 0)
    cols_other = swap_core(cols)
    encoded = unit_rows(jnp.dot(rows, enc, preferred_element_type=F32))
    encoded = jnp.stack([encoded, shift_z(encoded, -1), shift_z(encoded, 2), shift_z(encoded, 1)], 0)
    encoded_other = swap_core(encoded)
    pool = (jnp.arange(512)[None, :] // STEPS == jnp.arange(128)[:, None]).astype(BF16)
    state_cols = lax.dynamic_slice_in_dim(states, (zl * 2 + core) * 512, 512, 1)
    resid = jnp.dot(pool, state_cols, preferred_element_type=F32).astype(BF16)
    resid = jnp.dot(resid, proj, preferred_element_type=F32)
    w2 = down_proj(weights, cols, cols_other)
    w2 = (w2, shift(w2, "y", -1), shift(w2, "y", 2), shift(w2, "y", 1))
    hp = feed_forward(normed, part, other, weights)
    keep, send = embed(hp, w2, resid)
    emb = (keep + swap_core(send)).astype(BF16).reshape(8, 16, 1024)
    emb = lax.all_to_all(emb, ("zl", "zh"), 0, 0)
    cands = lax.all_to_all(candidates(emb), ("x", "y"), 0, 0).reshape(256, 1024)
    kernel, note = score(cands, encoded, encoded_other, ids)
    notes = lax.all_to_all(note, ("zl", "core", "zh"), 0, 0)
    partial = lax.all_to_all(vote(notes, kernel), ("zl", "core", "x", "y"), 0, 0)
    votes = jnp.sum(partial.reshape(8, 16, 16, 16), axis=1)
    return votes.transpose(1, 0, 2).reshape(16, 1, 128)


def solution(mesh):
    fine = Mesh(mesh.devices.reshape(4, 2, 4, 4, 2), ("zl", "core", "x", "y", "zh"))
    gen, user, cand = ("zl", "core"), ("x", "y"), "zh"
    return jax.shard_map(
        shards,
        mesh=fine,
        in_specs=(
            P(user + (cand,), None),
            P(),
            P(user, gen),
            P(user, gen),
            P(gen, user),
            P(gen, None),
            P(gen + user, None),
            P(),
            P(gen + user),
        ),
        out_specs=P(None, cand, None),
        check_vma=False,
    )
```

```python
import jax
import jax.numpy as jnp
from jax import lax
from jax.experimental import pallas as pl
from jax.experimental.pallas import tpu as pltpu
from jax.sharding import Mesh, PartitionSpec as P

STEPS = 4
CAP = 8
F32 = jnp.float32
BF16 = jnp.bfloat16
VMEM = pl.BlockSpec(memory_space=pltpu.VMEM)


def z_pairs(pairs):
    place = lambda z: (z % 4) * 2 + z // 4
    return [(place(a % 8), place(b % 8)) for a, b in pairs]


def shift_z(a, k):
    return lax.ppermute(a, ("zl", "zh"), z_pairs([(z, z + k) for z in range(8)]))


def send_z(a, pairs):
    return lax.ppermute(a, ("zl", "zh"), z_pairs(pairs))


def shift(a, axis, k):
    return lax.ppermute(a, axis, [(i, (i + k) % 4) for i in range(4)])


def swap_core(a):
    return lax.ppermute(a, "core", [(0, 1), (1, 0)])


def pack_kernel(gate, up, down, out):
    c = lax.axis_index("zh")
    full = pl.ds(pl.multiple_of(c * 512, 128), 384)
    out[0:256, 0:384] = gate[:, full]
    out[0:256, 384:768] = up[:, full]
    g = gate[:, 384:512].astype(F32)
    u = up[:, 384:512].astype(F32)
    g = jnp.where(c == 0, g, pltpu.roll(g, 64, 1))
    u = jnp.where(c == 0, pltpu.roll(u, 64, 1), u)
    lane = lax.broadcasted_iota(jnp.int32, (256, 128), 1)
    out[0:256, 768:896] = jnp.where(lane < 64, g, u).astype(BF16)
    for i in range(2):
        for j in range(7):
            start = 384 + c * 64 if j == 6 else c * 512 + j * 64
            rows = pl.ds(pl.multiple_of(start, 64), 64)
            out[256 + i * 64 : 320 + i * 64, j * 128 : (j + 1) * 128] = down[rows, i * 128 : (i + 1) * 128]


def pack_weights(gate, up, down):
    return pl.pallas_call(
        pack_kernel,
        out_shape=jax.ShapeDtypeStruct((384, 896), BF16),
        in_specs=[VMEM] * 3,
        out_specs=VMEM,
        name="pack_weights",
    )(gate, up, down)


def norm_kernel(states, gain, normed, mine, piece):
    zl, core = lax.axis_index("zl"), lax.axis_index("core")
    values = states[...].astype(F32)
    scale = lax.rsqrt(jnp.mean(values * values, axis=1, keepdims=True) + 1e-05)
    normed[...] = (values * scale * gain[...]).astype(BF16)
    part = normed[pl.ds(pl.multiple_of(core * 64, 64), 64), :]
    mine[0] = part

    @pl.when(pl.program_id(0) == 3 - zl)
    def _():
        piece[...] = part


def norm(states, gain):
    d = states.shape[1]
    return pl.pallas_call(
        norm_kernel,
        out_shape=(
            jax.ShapeDtypeStruct((512, d), BF16),
            jax.ShapeDtypeStruct((4, 64, d), BF16),
            jax.ShapeDtypeStruct((64, d), BF16),
        ),
        grid=(4,),
        in_specs=[
            pl.BlockSpec((128, d), lambda i: (i, 0)),
            pl.BlockSpec((1, d), lambda i: (0, 0)),
        ],
        out_specs=(
            pl.BlockSpec((128, d), lambda i: (i, 0)),
            pl.BlockSpec((1, 64, d), lambda i: (i, 0, 0)),
            pl.BlockSpec((64, d), lambda i: (0, 0)),
        ),
        name="norm",
    )(states, gain.reshape(1, d))


def exchange_states(mine, piece, cols, zl):
    piece, cols = lax.optimization_barrier((piece, cols))
    q = send_z(piece, [(z, 7 - z) for z in range(8)])
    near = (shift_z(cols, -1), shift_z(cols, 2), shift_z(cols, 1))
    q, near = lax.optimization_barrier((q, near))
    first, last = zl == 0, zl == 3
    p1 = shift_z(jnp.where(last, mine[2], q), 1)
    p2 = shift_z(jnp.where(first, mine[1], q), -1)
    p3 = send_z(jnp.where(last, mine[3], q), [(0, 2), (4, 6), (3, 4), (7, 0)])
    p4 = send_z(jnp.where(first, mine[0], q), [(3, 1), (7, 5), (0, 7), (4, 3)])
    return jnp.concatenate([q, p1, p2, p3 + p4], 0), jnp.stack([cols, *near], 0)


def places():
    zl, core, c = lax.axis_index("zl"), lax.axis_index("core"), lax.axis_index("zh")
    pieces = (
        zl,
        jnp.where(zl == 0, 2, zl - 1),
        jnp.where(zl == 3, 1, zl + 1),
        jnp.where(zl < 2, 3, 0),
    )
    own = [c * 8 + i for i in range(8)]
    part = [(1 - c) * 8 + p * 2 + core for p in pieces]
    other = [(1 - c) * 8 + p * 2 + 1 - core for p in pieces]
    return own + part + other


def ff_kernel(own, part, other, w_ref, hp_ref, acc):
    k = pl.program_id(0)
    w = jnp.concatenate([w_ref[i] for i in range(4)], axis=0)
    pairs = ((pl.ds(0, 512), own), (pl.ds(512, 256), part), (pl.ds(768, 256), other))

    @pl.when(k == 0)
    def _():
        for rows, tokens in pairs:
            acc[rows, :] = jnp.dot(tokens[...], w, preferred_element_type=F32)

    @pl.when(k > 0)
    def _():
        for rows, tokens in pairs:
            acc[rows, :] += jnp.dot(tokens[...], w, preferred_element_type=F32)

    @pl.when(k == 3)
    def _():
        row = lax.broadcasted_iota(jnp.int32, (64, 256), 0)
        col = lax.broadcasted_iota(jnp.int32, (64, 256), 1)
        pool = (col // STEPS == row).astype(BF16)
        lane = lax.broadcasted_iota(jnp.int32, (256, 128), 1)
        place = places()
        for j in range(4):
            at = pl.ds(j * 256, 256)
            gate = acc[at, 0:384]
            up = acc[at, 384:768]
            mixed = acc[at, 768:896]
            hidden = (jax.nn.silu(gate) * up).astype(BF16)
            rest = jnp.where(lane < 64, jax.nn.silu(mixed) * pltpu.roll(mixed, 64, 1), 0.0).astype(BF16)
            hp = jnp.dot(pool, hidden, preferred_element_type=F32).astype(BF16)
            hp_rest = jnp.dot(pool, rest, preferred_element_type=F32).astype(BF16)
            for t in range(4):
                to = pl.ds(pl.multiple_of(place[j * 4 + t] * 16, 16), 16)
                hp_ref[to, 0:384] = hp[t * 16 : (t + 1) * 16]
                hp_ref[to, 384:512] = hp_rest[t * 16 : (t + 1) * 16]


def feed_forward(own, part, other, weights):
    return pl.pallas_call(
        ff_kernel,
        out_shape=jax.ShapeDtypeStruct((256, 512), BF16),
        grid=(4,),
        in_specs=[
            pl.BlockSpec((512, 1024), lambda k: (0, k)),
            pl.BlockSpec((256, 1024), lambda k: (0, k)),
            pl.BlockSpec((256, 1024), lambda k: (0, k)),
            pl.BlockSpec((4, 256, 896), lambda k: (k, 0, 0)),
        ],
        out_specs=pl.BlockSpec((256, 512), lambda k: (0, 0)),
        scratch_shapes=[pltpu.VMEM((1024, 896), F32)],
        name="feed_forward",
    )(own, part, other, weights)


def w2_kernel(d_ref, mine, theirs, out, acc):
    x = pl.program_id(0)
    zl, core = lax.axis_index("zl"), lax.axis_index("core")
    rel = lax.rem(x - zl + 4, 4)
    ds, ps = [], []
    for y in range(4):
        for i in range(2):
            tiles = [d_ref[y, i * 64 : (i + 1) * 64, j * 128 : (j + 1) * 128] for j in range(7)]
            ds.append(jnp.concatenate(tiles, 0))
            col = slice(((y % 2) * 2 + i) * 256, ((y % 2) * 2 + i + 1) * 256)
            ps.append(jnp.where(core == y // 2, mine[rel, :, col], theirs[rel, :, col]))
    d = jnp.dot(jnp.concatenate(ds, 1), jnp.concatenate(ps, 0), preferred_element_type=F32)

    @pl.when(x == 0)
    def _():
        acc[...] = d

    @pl.when(x > 0)
    def _():
        acc[...] += d

    @pl.when(x == 3)
    def _():
        out[0:448, :] = acc[...].astype(BF16)
        out[448:512, :] = jnp.zeros((64, 256), BF16)


def down_proj(weights, mine, theirs):
    whole = pl.BlockSpec((4, 128, 1024), lambda k: (0, 0, 0))
    return pl.pallas_call(
        w2_kernel,
        out_shape=jax.ShapeDtypeStruct((512, 256), BF16),
        grid=(4,),
        in_specs=[pl.BlockSpec((4, 128, 896), lambda k: (k, 2, 0)), whole, whole],
        out_specs=pl.BlockSpec((512, 256), lambda k: (0, 0)),
        scratch_shapes=[pltpu.VMEM((448, 256), F32)],
        name="down_proj",
    )(weights, mine, theirs)


def embed_kernel(hp, w0, w1, w2, w3, resid, keep, send, emb):
    y, core, zh = lax.axis_index("y"), lax.axis_index("core"), lax.axis_index("zh")
    for k, w in enumerate((w0, w1, w2, w3)):
        col = pl.ds(pl.multiple_of(lax.rem(y + k, 4) * 256, 256), 256)
        emb[:, col] = jnp.dot(hp[...], w[...], preferred_element_type=F32)
    half = pl.ds(pl.multiple_of(zh * 128, 128), 128)
    emb[half, :] += resid[...]
    for z in range(4):
        for c in range(2):
            at = pl.ds((z * 2 + c) * 16, 16)
            base = c * 128 + z * 32
            keep[at, :] = emb[pl.ds(pl.multiple_of(base + core * 16, 16), 16), :] * (1.0 / STEPS)
            send[at, :] = emb[pl.ds(pl.multiple_of(base + 16 - core * 16, 16), 16), :] * (1.0 / STEPS)


def embed(hp, parts, resid):
    shape = jax.ShapeDtypeStruct((128, 1024), F32)
    return pl.pallas_call(
        embed_kernel,
        out_shape=(shape, shape),
        in_specs=[VMEM] * 6,
        out_specs=(VMEM, VMEM),
        scratch_shapes=[pltpu.VMEM((256, 1024), F32)],
        name="embed",
    )(hp, *parts, resid)


def unit_rows(matrix):
    return (matrix * lax.rsqrt(jnp.sum(matrix * matrix, axis=1, keepdims=True) + 1e-06)).astype(BF16)


def candidate_kernel(parts, out):
    total = parts[0].astype(F32)
    for i in range(1, 8):
        total += parts[i].astype(F32)
    cand = unit_rows(total)
    for i in range(16):
        out[i] = cand


def candidates(parts):
    return pl.pallas_call(
        candidate_kernel,
        out_shape=jax.ShapeDtypeStruct((16, 16, 1024), BF16),
        in_specs=[VMEM],
        out_specs=VMEM,
        name="candidates",
    )(parts)


def row_of(b):
    k, s = b % 4, b // 4
    core = lax.axis_index("core")
    core = core if s == 0 else 1 - core
    return lax.rem(lax.axis_index("zl") + k, 4) * 2 + core


def score_kernel(cands, mine, theirs, ids_row, ids_col, kernel_ref, note_ref, note):
    match = (ids_row[...] == ids_col[...]).astype(F32)
    count = jnp.sum(match, axis=0, keepdims=True)
    note[8:16, :] = jnp.broadcast_to(jnp.minimum(1.0, CAP / count), (8, 256))
    for b in range(8):
        rows = (mine if b < 4 else theirs)[b % 4]
        scores = lax.dot_general(
            cands[...], rows, (((1,), (1,)), ((), ())), preferred_element_type=F32
        )
        kernel = jnp.exp(scores * 60.0)
        kernel_ref[:, b * 256 : (b + 1) * 256] = kernel
        note[pl.ds(row_of(b), 1), :] = jnp.sum(kernel, axis=0, keepdims=True)
    for i in range(16):
        note_ref[i] = note[...]


def score(cands, mine, theirs, ids):
    return pl.pallas_call(
        score_kernel,
        out_shape=(
            jax.ShapeDtypeStruct((256, 2048), F32),
            jax.ShapeDtypeStruct((16, 16, 256), F32),
        ),
        in_specs=[VMEM] * 5,
        out_specs=(VMEM, VMEM),
        scratch_shapes=[pltpu.VMEM((16, 256), F32)],
        name="score",
    )(cands, mine, theirs, ids.reshape(1, 256), ids.reshape(256, 1))


def vote_kernel(notes, kernel, out, weight):
    totals = notes[0, 0:8, :]
    for i in range(1, 16):
        totals += notes[i, 0:8, :]
    for r in range(8):
        weight[r : r + 1, :] = notes[2 * r, 8:9, :] / totals[r : r + 1] * (4096 / 32768)
    acc = None
    for b in range(8):
        w = weight[pl.ds(row_of(b), 1), :]
        part = kernel[:, b * 256 : (b + 1) * 256] * w
        acc = part if acc is None else acc + part
    votes = jnp.sum(acc.T, axis=0, keepdims=True)
    pair = jnp.concatenate([votes[:, :128], votes[:, 128:]], 0)
    out[...] = jnp.broadcast_to(pair[None], (128, 2, 128))


def vote(notes, kernel):
    return pl.pallas_call(
        vote_kernel,
        out_shape=jax.ShapeDtypeStruct((128, 2, 128), F32),
        in_specs=[VMEM, VMEM],
        out_specs=VMEM,
        scratch_shapes=[pltpu.VMEM((8, 256), F32)],
        name="vote",
    )(notes, kernel)


def shards(states, norm_gain, gate, up, down, proj, rows, enc, ids):
    zl, core, y = lax.axis_index("zl"), lax.axis_index("core"), lax.axis_index("y")
    weights = lax.all_gather(pack_weights(gate, up, down), ("x", "y"), axis=0)
    normed, mine, piece = norm(states, norm_gain)
    cols = lax.dynamic_slice_in_dim(proj, y * 256, 256, 1)
    cols = jnp.concatenate([cols[i * 128 : (i + 1) * 128] for i in range(4)], axis=1)
    part, cols = exchange_states(mine, piece, cols, zl)
    pool = (jnp.arange(512)[None, :] // STEPS == jnp.arange(128)[:, None]).astype(BF16)
    state_cols = lax.dynamic_slice_in_dim(states, (zl * 2 + core) * 512, 512, 1)
    resid = jnp.dot(pool, state_cols, preferred_element_type=F32).astype(BF16)
    resid = jnp.dot(resid, proj, preferred_element_type=F32)
    encoded = unit_rows(jnp.dot(rows, enc, preferred_element_type=F32))
    part, cols, resid, encoded = lax.optimization_barrier((part, cols, resid, encoded))
    other = swap_core(part)
    cols_other = swap_core(cols)
    near = []
    for k in (-1, 2, 1):
        near.append(shift_z(encoded, k))
    w2 = down_proj(weights, cols, cols_other)
    w2 = (w2, shift(w2, "y", -1), shift(w2, "y", 2), shift(w2, "y", 1))
    hp = feed_forward(normed, part, other, weights)
    keep, send = embed(hp, w2, resid)
    emb = (keep + swap_core(send)).astype(BF16).reshape(8, 16, 1024)
    emb = lax.all_to_all(emb, ("zl", "zh"), 0, 0)
    cands, near = lax.optimization_barrier((candidates(emb), near))
    encoded = jnp.stack([encoded, *near], 0)
    encoded_other = swap_core(encoded)
    cands = lax.all_to_all(cands, ("x", "y"), 0, 0).reshape(256, 1024)
    kernel, note = score(cands, encoded, encoded_other, ids)
    notes = lax.all_to_all(note, ("zl", "core", "zh"), 0, 0)
    partial = lax.all_to_all(vote(notes, kernel), ("zl", "core", "x", "y"), 0, 0)
    votes = jnp.sum(partial.reshape(8, 16, 16, 16), axis=1)
    return votes.transpose(1, 0, 2).reshape(16, 1, 128)


def solution(mesh):
    fine = Mesh(mesh.devices.reshape(4, 2, 4, 4, 2), ("zl", "core", "x", "y", "zh"))
    gen, user, cand = ("zl", "core"), ("x", "y"), "zh"

    return jax.shard_map(
        shards,
        mesh=fine,
        in_specs=(
            P(user + (cand,), None),
            P(),
            P(user, gen),
            P(user, gen),
            P(gen, user),
            P(gen, None),
            P(gen + user, None),
            P(),
            P(gen + user),
        ),
        out_specs=P(None, cand, None),
        check_vma=False,
    )
```

```python
import functools

import functools

import jax
import jax.numpy as jnp
from jax import lax
from jax.experimental import pallas as pl
from jax.experimental.pallas import tpu as pltpu
from jax.sharding import Mesh, PartitionSpec as P

STEPS = 4
CAP = 8
F32 = jnp.float32
BF16 = jnp.bfloat16
VMEM = pl.BlockSpec(memory_space=pltpu.VMEM)


def z_pairs(pairs):
    place = lambda z: (z % 4) * 2 + z // 4
    return [(place(a % 8), place(b % 8)) for a, b in pairs]


def shift_z(a, k):
    return lax.ppermute(a, ("zl", "zh"), z_pairs([(z, z + k) for z in range(8)]))


def send_z(a, pairs):
    return lax.ppermute(a, ("zl", "zh"), z_pairs(pairs))


def shift(a, axis, k):
    return lax.ppermute(a, axis, [(i, (i + k) % 4) for i in range(4)])


def swap_core(a):
    return lax.ppermute(a, "core", [(0, 1), (1, 0)])


def pack_kernel(gate, up, down, *outs):
    c = lax.axis_index("zh")
    full = pl.ds(pl.multiple_of(c * 512, 128), 384)
    g = gate[:, 384:512].astype(F32)
    u = up[:, 384:512].astype(F32)
    g = jnp.where(c == 0, g, pltpu.roll(g, 64, 1))
    u = jnp.where(c == 0, pltpu.roll(u, 64, 1), u)
    lane = lax.broadcasted_iota(jnp.int32, (256, 128), 1)
    last = jnp.where(lane < 64, g, u).astype(BF16)
    for i, out in enumerate(outs):
        at = slice(i * 128, (i + 1) * 128)
        out[0:128, 0:384] = gate[at, full]
        out[0:128, 384:768] = up[at, full]
        out[0:128, 768:896] = last[at]
        for j in range(7):
            start = 384 + c * 64 if j == 6 else c * 512 + j * 64
            rows = pl.ds(pl.multiple_of(start, 64), 64)
            out[128:192, j * 128 : (j + 1) * 128] = down[rows, at]


def pack_weights(gate, up, down):
    return pl.pallas_call(
        pack_kernel,
        out_shape=(jax.ShapeDtypeStruct((192, 896), BF16),) * 2,
        in_specs=[VMEM] * 3,
        out_specs=(VMEM,) * 2,
        name="pack_weights",
    )(gate, up, down)


def spread_first(chunk, axis):
    got = []
    for k in (-1, 2, 1):
        got.append(shift(chunk, axis, k))
    return got


def normed_rows(states, gain):
    values = states.astype(F32)
    scale = lax.rsqrt(jnp.mean(values * values, axis=1, keepdims=True) + 1e-05)
    return (values * scale * gain).astype(BF16)


def piece_kernel(which, states, gain, piece, rest):
    rest[0] = normed_rows(states[...], gain[...])

    @pl.when(pl.program_id(0) == 0)
    def _():
        piece[...] = rest[0]


def norm_pieces(states, gain, which):
    d = states.shape[1]
    return pl.pallas_call(
        piece_kernel,
        out_shape=(jax.ShapeDtypeStruct((64, d), BF16), jax.ShapeDtypeStruct((2, 64, d), BF16)),
        grid_spec=pltpu.PrefetchScalarGridSpec(
            num_scalar_prefetch=1,
            grid=(3,),
            in_specs=[
                pl.BlockSpec((64, d), lambda i, w: (w[i], 0)),
                pl.BlockSpec((1, d), lambda i, w: (0, 0)),
            ],
            out_specs=(
                pl.BlockSpec((64, d), lambda i, w: (0, 0)),
                pl.BlockSpec((1, 64, d), lambda i, w: (jnp.maximum(i - 1, 0), 0, 0)),
            ),
        ),
        name="norm_pieces",
    )(which, states, gain.reshape(1, d))


def norm_kernel(states, gain, normed):
    normed[...] = normed_rows(states[...], gain[...])


def norm(states, gain):
    d = states.shape[1]
    return pl.pallas_call(
        norm_kernel,
        out_shape=jax.ShapeDtypeStruct((512, d), BF16),
        grid=(4,),
        in_specs=[
            pl.BlockSpec((128, d), lambda i: (i, 0)),
            pl.BlockSpec((1, d), lambda i: (0, 0)),
        ],
        out_specs=pl.BlockSpec((128, d), lambda i: (i, 0)),
        name="norm",
    )(states, gain.reshape(1, d))


def exchange_states(rest, q, zl):
    first, last = zl == 0, zl == 3
    up, dn = jnp.where(last, rest[0], q), jnp.where(first, rest[0], q)
    up2, dn2 = jnp.where(last, rest[1], q), jnp.where(first, rest[1], q)
    up, dn, up2, dn2 = lax.optimization_barrier((up, dn, up2, dn2))
    p1 = shift_z(up, 1)
    p2 = shift_z(dn, -1)
    p3 = send_z(up2, [(0, 2), (4, 6), (3, 4), (7, 0)])
    p4 = send_z(dn2, [(3, 1), (7, 5), (0, 7), (4, 3)])
    return jnp.concatenate([q, p1, p2, p3 + p4], 0)


def places():
    zl, core, c = lax.axis_index("zl"), lax.axis_index("core"), lax.axis_index("zh")
    pieces = (
        zl,
        jnp.where(zl == 0, 2, zl - 1),
        jnp.where(zl == 3, 1, zl + 1),
        jnp.where(zl < 2, 3, 0),
    )
    own = [c * 8 + i for i in range(8)]
    part = [(1 - c) * 8 + p * 2 + core for p in pieces]
    other = [(1 - c) * 8 + p * 2 + 1 - core for p in pieces]
    return own + part + other


def user_of(colour, m, k):
    x, y = lax.axis_index("x"), lax.axis_index("y")
    if colour == 0:
        return lax.rem(x + k, 4), lax.rem(y + m, 4)
    return lax.rem(x + m, 4), lax.rem(y + k, 4)


def ff_kernel(spec, own, part, other, *refs):
    n = 2 * len(spec)
    bundles, refs = refs[:n], refs[n:]
    hp_ref, tok, acc, sems = refs[:4]
    held = refs[4:]
    copies = [
        pltpu.make_async_copy(b.at[:, pl.ds(0, 128)], held[i // 2].at[pl.ds(i % 2 * 2, 2)], sems.at[i])
        for i, b in enumerate(bundles)
    ]
    toks = [
        pltpu.make_async_copy(own, tok.at[0], sems.at[n]),
        pltpu.make_async_copy(part, tok.at[1, pl.ds(0, 256)], sems.at[n + 1]),
        pltpu.make_async_copy(other, tok.at[1, pl.ds(256, 256)], sems.at[n + 2]),
    ]
    copies[0].start()
    copies[1].start()
    toks[0].start()
    for copy in copies[2:] + toks[1:]:
        copy.start()
    toks[0].wait()
    place = places()
    row = lax.broadcasted_iota(jnp.int32, (64, 256), 0)
    col = lax.broadcasted_iota(jnp.int32, (64, 256), 1)
    pool = (col // STEPS == row).astype(BF16)
    lane = lax.broadcasted_iota(jnp.int32, (256, 128), 1)

    def rows(i, _):
        @pl.when(i == 1)
        def _():
            toks[1].wait()
            toks[2].wait()

        for b, (colour, m) in enumerate(spec):
            pl.when(i == 0)(copies[2 * b].wait)
            pl.when(i == 0)(copies[2 * b + 1].wait)
            xs, ws = [], []
            for k in range(4):
                ux, uy = user_of(colour, m, k)
                at = pl.multiple_of((ux * 4 + uy) * 256 + colour * 128, 128)
                xs.append(tok[i, :, pl.ds(at, 128)])
                ws.append(held[b][k])
            d = jnp.dot(jnp.concatenate(xs, 1), jnp.concatenate(ws, 0), preferred_element_type=F32)
            if b == 0:
                acc[...] = d
            else:
                acc[...] += d
        for j in range(2):
            at = slice(j * 256, (j + 1) * 256)
            gate = acc[at, 0:384]
            up = acc[at, 384:768]
            mixed = acc[at, 768:896]
            hidden = (jax.nn.silu(gate) * up).astype(BF16)
            rest = jnp.where(lane < 64, jax.nn.silu(mixed) * pltpu.roll(mixed, 64, 1), 0.0).astype(BF16)
            hp = jnp.dot(pool, hidden, preferred_element_type=F32).astype(BF16)
            hp_rest = jnp.dot(pool, rest, preferred_element_type=F32).astype(BF16)
            for t in range(4):
                to = jnp.where(i == 0, place[j * 4 + t], place[8 + j * 4 + t])
                to = pl.ds(pl.multiple_of(to * 16, 16), 16)
                hp_ref[to, 0:384] = hp[t * 16 : (t + 1) * 16]
                hp_ref[to, 384:512] = hp_rest[t * 16 : (t + 1) * 16]
        return 0

    lax.fori_loop(0, 2, rows, 0)


def feed_forward(spec, own, part, other, bundles):
    args = (own, part, other, *bundles)
    return pl.pallas_call(
        functools.partial(ff_kernel, spec),
        out_shape=jax.ShapeDtypeStruct((256, 512), BF16),
        in_specs=[pl.BlockSpec(memory_space=pl.ANY)] * len(args),
        out_specs=VMEM,
        scratch_shapes=[
            pltpu.VMEM((2, 512, 4096), BF16),
            pltpu.VMEM((512, 896), F32),
            pltpu.SemaphoreType.DMA((2 * len(spec) + 3,)),
        ]
        + [pltpu.VMEM((4, 128, 896), BF16) for _ in spec],
        name="feed_forward",
    )(*args)


def w2_kernel(spec, mine, theirs, *refs):
    bundles, out = refs[:-1], refs[-1]
    zl, core = lax.axis_index("zl"), lax.axis_index("core")
    acc = None
    for b, (colour, m) in enumerate(spec):
        ds, ps = [], []
        for k in range(4):
            ux, uy = user_of(colour, m, k)
            ds.append(jnp.concatenate([bundles[2 * b + k // 2][k % 2, :, j * 128 : (j + 1) * 128] for j in range(7)], 0))
            rel = lax.rem(ux - zl + 4, 4)
            col = pl.ds(pl.multiple_of((lax.rem(uy, 2) * 2 + colour) * 256, 256), 256)
            ps.append(jnp.where(uy // 2 == core, mine[rel, :, col], theirs[rel, :, col]))
        d = jnp.dot(jnp.concatenate(ds, 1), jnp.concatenate(ps, 0), preferred_element_type=F32)
        acc = d if acc is None else acc + d
    out[0:448, :] = acc.astype(BF16)
    out[448:512, :] = jnp.zeros((64, 256), BF16)


def down_proj(spec, mine, theirs, bundles):
    whole = pl.BlockSpec((4, 128, 1024), lambda i: (0, 0, 0))
    return pl.pallas_call(
        functools.partial(w2_kernel, spec),
        out_shape=jax.ShapeDtypeStruct((512, 256), BF16),
        grid=(1,),
        in_specs=[whole, whole] + [pl.BlockSpec((b.shape[0], 64, 896), lambda i: (0, 2, 0)) for b in bundles],
        out_specs=pl.BlockSpec((512, 256), lambda i: (0, 0)),
        name="down_proj",
    )(mine, theirs, *bundles)


def embed_kernel(hp, w0, w1, w2, w3, resid, keep, send, emb):
    y, core, zh = lax.axis_index("y"), lax.axis_index("core"), lax.axis_index("zh")
    for k, w in enumerate((w0, w1, w2, w3)):
        col = pl.ds(pl.multiple_of(lax.rem(y + k, 4) * 256, 256), 256)
        emb[:, col] = jnp.dot(hp[...], w[...], preferred_element_type=F32)
    half = pl.ds(pl.multiple_of(zh * 128, 128), 128)
    emb[half, :] += resid[...]
    for z in range(4):
        for c in range(2):
            at = pl.ds((z * 2 + c) * 16, 16)
            base = c * 128 + z * 32
            keep[at, :] = emb[pl.ds(pl.multiple_of(base + core * 16, 16), 16), :] * (1.0 / STEPS)
            send[at, :] = emb[pl.ds(pl.multiple_of(base + 16 - core * 16, 16), 16), :] * (1.0 / STEPS)


def embed(hp, parts, resid):
    shape = jax.ShapeDtypeStruct((128, 1024), F32)
    return pl.pallas_call(
        embed_kernel,
        out_shape=(shape, shape),
        in_specs=[VMEM] * 6,
        out_specs=(VMEM, VMEM),
        scratch_shapes=[pltpu.VMEM((256, 1024), F32)],
        name="embed",
    )(hp, *parts, resid)


def unit_rows(matrix):
    return (matrix * lax.rsqrt(jnp.sum(matrix * matrix, axis=1, keepdims=True) + 1e-06)).astype(BF16)


def candidate_kernel(parts, out):
    total = parts[0].astype(F32)
    for i in range(1, 8):
        total += parts[i].astype(F32)
    cand = unit_rows(total)
    for i in range(16):
        out[i] = cand


def candidates(parts):
    return pl.pallas_call(
        candidate_kernel,
        out_shape=jax.ShapeDtypeStruct((16, 16, 1024), BF16),
        in_specs=[VMEM],
        out_specs=VMEM,
        name="candidates",
    )(parts)


def row_of(k, s):
    core = lax.axis_index("core")
    core = core if s == 0 else 1 - core
    return lax.rem(lax.axis_index("zl") + k, 4) * 2 + core


def score_kernel(cands, mine, theirs, ids_row, ids_col, kernel_ref, note_ref, note):
    match = (ids_row[...] == ids_col[...]).astype(F32)
    count = jnp.sum(match, axis=0, keepdims=True)
    note[8:16, :] = jnp.broadcast_to(jnp.minimum(1.0, CAP / count), (8, 256))

    def block(k, _):
        for s, rows in enumerate((mine, theirs)):
            scores = lax.dot_general(
                cands[...], rows[k], (((1,), (1,)), ((), ())), preferred_element_type=F32
            )
            kernel = jnp.exp(scores * 60.0)
            kernel_ref[:, pl.ds(pl.multiple_of(s * 1024 + k * 256, 256), 256)] = kernel
            note[pl.ds(row_of(k, s), 1), :] = jnp.sum(kernel, axis=0, keepdims=True)
        return 0

    lax.fori_loop(0, 4, block, 0)
    for i in range(16):
        note_ref[i] = note[...]


def score(cands, mine, theirs, ids):
    return pl.pallas_call(
        score_kernel,
        out_shape=(
            jax.ShapeDtypeStruct((256, 2048), F32),
            jax.ShapeDtypeStruct((16, 16, 256), F32),
        ),
        in_specs=[VMEM] * 5,
        out_specs=(VMEM, VMEM),
        scratch_shapes=[pltpu.VMEM((16, 256), F32)],
        name="score",
    )(cands, mine, theirs, ids.reshape(1, 256), ids.reshape(256, 1))


def vote_kernel(notes, kernel, out, weight):
    totals = notes[0, 0:8, :]
    for i in range(1, 16):
        totals += notes[i, 0:8, :]
    for r in range(8):
        weight[r : r + 1, :] = notes[2 * r, 8:9, :] / totals[r : r + 1] * (4096 / 32768)
    acc = None
    for b in range(8):
        w = weight[pl.ds(row_of(b % 4, b // 4), 1), :]
        part = kernel[:, b * 256 : (b + 1) * 256] * w
        acc = part if acc is None else acc + part
    votes = jnp.sum(acc.T, axis=0, keepdims=True)
    pair = jnp.concatenate([votes[:, :128], votes[:, 128:]], 0)
    out[...] = jnp.broadcast_to(pair[None], (128, 2, 128))


def vote(notes, kernel):
    return pl.pallas_call(
        vote_kernel,
        out_shape=jax.ShapeDtypeStruct((128, 2, 128), F32),
        in_specs=[VMEM, VMEM],
        out_specs=VMEM,
        scratch_shapes=[pltpu.VMEM((8, 256), F32)],
        name="vote",
    )(notes, kernel)


BUNDLES = tuple((colour, m) for colour in range(2) for m in (0, 1, 3)) + tuple((colour, 2) for colour in range(2))


def shards(states, norm_gain, gate, up, down, proj, rows, enc, ids):
    zl, core, y = lax.axis_index("zl"), lax.axis_index("core"), lax.axis_index("y")
    ends = jnp.stack([3 - zl, jnp.where(zl == 3, 2, 1), jnp.where(zl == 3, 3, 0)])
    piece, rest = norm_pieces(states, norm_gain, ends * 2 + core)
    a, b, piece = lax.optimization_barrier((*pack_weights(gate, up, down), piece))
    q = send_z(piece, [(z, 7 - z) for z in range(8)])
    near_a = spread_first(a, "x")
    near_b = spread_first(b, "y")
    cols = lax.dynamic_slice_in_dim(proj, y * 256, 256, 1)
    cols = jnp.concatenate([cols[i * 128 : (i + 1) * 128] for i in range(4)], axis=1)
    near_cols = []
    for k in (-1, 2, 1):
        near_cols.append(shift_z(cols, k))
    normed = norm(states, norm_gain)
    a_lo, a_hi, b_lo, b_hi = lax.optimization_barrier(
        (
            jnp.stack([a, near_a[0]], 0),
            jnp.stack([near_a[1], near_a[2]], 0),
            jnp.stack([b, near_b[0]], 0),
            jnp.stack([near_b[1], near_b[2]], 0),
        )
    )
    moves = [(a_lo, "y", 1), (a_hi, "y", -1), (b_lo, "x", 1), (b_hi, "x", -1)]
    moves += [(a_hi, "y", 1), (a_lo, "y", -1), (b_hi, "x", 1), (b_lo, "x", -1)]
    got = []
    for bundle, axis, k in moves:
        got.append(shift(bundle, axis, k))
    near = (a_lo, a_hi, got[5], got[1], got[0], got[4], b_lo, b_hi, got[7], got[3], got[2], got[6])
    part = exchange_states(rest, q, zl)
    pool = (jnp.arange(512)[None, :] // STEPS == jnp.arange(128)[:, None]).astype(BF16)
    state_cols = lax.dynamic_slice_in_dim(states, (zl * 2 + core) * 512, 512, 1)
    resid = jnp.dot(pool, state_cols, preferred_element_type=F32).astype(BF16)
    resid = jnp.dot(resid, proj, preferred_element_type=F32)
    encoded = unit_rows(jnp.dot(rows, enc, preferred_element_type=F32))
    cols, *near_cols = lax.optimization_barrier((cols, *near_cols))
    cols = jnp.stack([cols, *near_cols], 0)
    cols_other = swap_core(cols)
    far = []
    for i, (_, axis, k) in enumerate(moves[:4]):
        far.append(shift(got[i], axis, k))
    part, resid, encoded = lax.optimization_barrier((part, resid, encoded))
    other = swap_core(part)
    near_rows = []
    for k in (-1, 2, 1):
        near_rows.append(shift_z(encoded, k))
    bundles = near + tuple(far)
    w2 = down_proj(BUNDLES, cols, cols_other, bundles)
    parts = [w2]
    for k in (-1, 2, 1):
        parts.append(shift(w2, "y", k))
    hp = feed_forward(BUNDLES, normed, part, other, bundles)
    keep, send = embed(hp, parts, resid)
    emb = (keep + swap_core(send)).astype(BF16).reshape(8, 16, 1024)
    emb = lax.all_to_all(emb, ("zl", "zh"), 0, 0)
    cands, near = lax.optimization_barrier((candidates(emb), near_rows))
    encoded = jnp.stack([encoded, *near_rows], 0)
    encoded_other = swap_core(encoded)
    cands = lax.all_to_all(cands, ("x", "y"), 0, 0).reshape(256, 1024)
    kernel, note = score(cands, encoded, encoded_other, ids)
    notes = lax.all_to_all(note, ("zl", "core", "zh"), 0, 0)
    partial = lax.all_to_all(vote(notes, kernel), ("zl", "core", "x", "y"), 0, 0)
    votes = jnp.sum(partial.reshape(8, 16, 16, 16), axis=1)
    return votes.transpose(1, 0, 2).reshape(16, 1, 128)


def solution(mesh):
    fine = Mesh(mesh.devices.reshape(4, 2, 4, 4, 2), ("zl", "core", "x", "y", "zh"))
    gen, user, cand = ("zl", "core"), ("x", "y"), "zh"

    return jax.shard_map(
        shards,
        mesh=fine,
        in_specs=(
            P(user + (cand,), None),
            P(),
            P(user, gen),
            P(user, gen),
            P(gen, user),
            P(gen, None),
            P(gen + user, None),
            P(),
            P(gen + user),
        ),
        out_specs=P(None, cand, None),
        check_vma=False,
    )
```

```python
import functools

import functools

import jax
import jax.numpy as jnp
from jax import lax
from jax.experimental import pallas as pl
from jax.experimental.pallas import tpu as pltpu
from jax.sharding import Mesh, PartitionSpec as P

STEPS = 4
CAP = 8
F32 = jnp.float32
BF16 = jnp.bfloat16
VMEM = pl.BlockSpec(memory_space=pltpu.VMEM)
ANY = pl.BlockSpec(memory_space=pl.ANY)


def z_pairs(pairs):
    place = lambda z: (z % 4) * 2 + z // 4
    return [(place(a % 8), place(b % 8)) for a, b in pairs]


def shift_z(a, k):
    return lax.ppermute(a, ("zl", "zh"), z_pairs([(z, z + k) for z in range(8)]))


def send_z(a, pairs):
    return lax.ppermute(a, ("zl", "zh"), z_pairs(pairs))


def shift(a, axis, k):
    return lax.ppermute(a, axis, [(i, (i + k) % 4) for i in range(4)])


def swap_core(a):
    return lax.ppermute(a, "core", [(0, 1), (1, 0)])


def pack_kernel(gate, up, down, gain, states, out_a, out_b, piece, sem):
    c, zl, core = lax.axis_index("zh"), lax.axis_index("zl"), lax.axis_index("core")
    user = lax.axis_index("x") * 4 + lax.axis_index("y")
    start = pl.multiple_of((3 - zl) * 128 + core * 64, 64)
    copy = pltpu.make_async_copy(states.at[pl.ds(start, 64)], piece, sem)
    copy.start()
    full = pl.ds(pl.multiple_of(c * 512, 128), 384)
    lane = lax.broadcasted_iota(jnp.int32, (128, 128), 1)
    for i, out in enumerate((out_a, out_b)):
        at = slice(i * 128, (i + 1) * 128)
        scale = jnp.broadcast_to(gain[pl.ds(user * 2 + i, 1), :], (128, 128)).T
        wide = jnp.concatenate([scale] * 3, 1)
        out[0:128, 0:384] = (gate[at, full].astype(F32) * wide).astype(BF16)
        out[0:128, 384:768] = (up[at, full].astype(F32) * wide).astype(BF16)
        g = gate[at, 384:512].astype(F32)
        u = up[at, 384:512].astype(F32)
        g = jnp.where(c == 0, g, pltpu.roll(g, 64, 1))
        u = jnp.where(c == 0, pltpu.roll(u, 64, 1), u)
        out[0:128, 768:896] = (jnp.where(lane < 64, g, u) * scale).astype(BF16)
        for j in range(7):
            first = 384 + c * 64 if j == 6 else c * 512 + j * 64
            rows = pl.ds(pl.multiple_of(first, 64), 64)
            out[128:192, j * 128 : (j + 1) * 128] = down[rows, at]
    copy.wait()


def pack_weights(gate, up, down, gain, states):
    d = states.shape[1]
    return pl.pallas_call(
        pack_kernel,
        out_shape=(jax.ShapeDtypeStruct((192, 896), BF16),) * 2 + (jax.ShapeDtypeStruct((64, d), BF16),),
        in_specs=[VMEM] * 4 + [ANY],
        out_specs=(VMEM,) * 3,
        scratch_shapes=[pltpu.SemaphoreType.DMA],
        name="pack_weights",
    )(gate, up, down, gain.reshape(d // 128, 128), states)


def run_copies(copies):
    for copy in copies:
        copy.start()
    for copy in copies:
        copy.wait()


def stack_kernel(groups, *refs):
    n = sum(groups)
    ins, outs, sems = refs[:n], refs[n:-1], refs[-1]
    copies, at = [], 0
    for size, out in zip(groups, outs):
        for k in range(size):
            copies.append(pltpu.make_async_copy(ins[at], out.at[k], sems.at[at]))
            at += 1
    run_copies(copies)


def stacks(*groups):
    arrays = [a for group in groups for a in group]
    out = tuple(jax.ShapeDtypeStruct((len(g),) + g[0].shape, g[0].dtype) for g in groups)
    return pl.pallas_call(
        functools.partial(stack_kernel, tuple(len(g) for g in groups)),
        out_shape=out,
        in_specs=[ANY] * len(arrays),
        out_specs=(VMEM,) * len(groups),
        scratch_shapes=[pltpu.SemaphoreType.DMA((len(arrays),))],
        name="stacks",
    )(*arrays)


def spread_first(chunk, axis):
    got = []
    for k in (-1, 2, 1):
        got.append(shift(chunk, axis, k))
    return got


def relay_kernel(states, q, *refs):
    outs, sems = refs[:4], refs[4]
    zl, core = lax.axis_index("zl"), lax.axis_index("core")
    for i, (out, end, piece) in enumerate(zip(outs, (3, 0, 3, 0), (2, 1, 3, 0))):
        own = states.at[pl.ds(pl.multiple_of(piece * 128 + core * 64, 64), 64)]
        pl.when(zl == end)(pltpu.make_async_copy(own, out, sems.at[i]).start)
        pl.when(zl != end)(pltpu.make_async_copy(q, out, sems.at[i]).start)
    for i, out in enumerate(outs):
        pltpu.make_async_copy(q, out, sems.at[i]).wait()


def join_kernel(q, p1, p2, p3, p4, out, sems):
    zl = lax.axis_index("zl")
    for i, p in enumerate((q, p1, p2)):
        pltpu.make_async_copy(p, out.at[pl.ds(i * 64, 64)], sems.at[i]).start()
    to = out.at[pl.ds(192, 64)]
    even = lax.rem(zl, 2) == 0
    pl.when(even)(pltpu.make_async_copy(p3, to, sems.at[3]).start)
    pl.when(jnp.logical_not(even))(pltpu.make_async_copy(p4, to, sems.at[3]).start)
    for i in range(4):
        pltpu.make_async_copy(q, out.at[pl.ds(i * 64, 64)], sems.at[i]).wait()


def exchange_states(states, q):
    sent = jax.ShapeDtypeStruct(q.shape, q.dtype)
    up, dn, up2, dn2 = pl.pallas_call(
        relay_kernel,
        out_shape=(sent,) * 4,
        in_specs=[ANY] * 2,
        out_specs=(VMEM,) * 4,
        scratch_shapes=[pltpu.SemaphoreType.DMA((4,))],
        name="relay",
    )(states, q)
    p1 = shift_z(up, 1)
    p2 = shift_z(dn, -1)
    p3 = send_z(up2, [(0, 2), (4, 6), (3, 4), (7, 0)])
    p4 = send_z(dn2, [(3, 1), (7, 5), (0, 7), (4, 3)])
    return pl.pallas_call(
        join_kernel,
        out_shape=jax.ShapeDtypeStruct((256, q.shape[1]), q.dtype),
        in_specs=[ANY] * 5,
        out_specs=VMEM,
        scratch_shapes=[pltpu.SemaphoreType.DMA((4,))],
        name="join",
    )(q, p1, p2, p3, p4)


def places():
    zl, core, c = lax.axis_index("zl"), lax.axis_index("core"), lax.axis_index("zh")
    pieces = (
        zl,
        jnp.where(zl == 0, 2, zl - 1),
        jnp.where(zl == 3, 1, zl + 1),
        jnp.where(zl < 2, 3, 0),
    )
    own = [c * 8 + i for i in range(8)]
    part = [(1 - c) * 8 + p * 2 + core for p in pieces]
    other = [(1 - c) * 8 + p * 2 + 1 - core for p in pieces]
    return own + part + other


def user_of(colour, m, k):
    x, y = lax.axis_index("x"), lax.axis_index("y")
    if isinstance(colour, int):
        dx, dy = (k, m) if colour == 0 else (m, k)
    else:
        dx, dy = jnp.where(colour == 0, k, m), jnp.where(colour == 0, m, k)
    return lax.rem(x + dx, 4), lax.rem(y + dy, 4)


def ff_kernel(own, part, other, *refs):
    n = 4 * len(ORDER)
    bundles, refs = refs[:n], refs[n:]
    hp_ref, tok, acc, squares, held, sems = refs
    copies = [
        pltpu.make_async_copy(b.at[:, pl.ds(0, 128)], held.at[i // 2, pl.ds(i % 2 * 2, 2)], sems.at[i])
        for i, b in enumerate(bundles)
    ]
    toks = [
        pltpu.make_async_copy(own, tok.at[0], sems.at[n]),
        pltpu.make_async_copy(part, tok.at[1, pl.ds(0, 256)], sems.at[n + 1]),
        pltpu.make_async_copy(other, tok.at[1, pl.ds(256, 256)], sems.at[n + 2]),
    ]
    toks[0].start()
    for copy in copies + toks[1:]:
        copy.start()
    place = places()
    row = lax.broadcasted_iota(jnp.int32, (64, 256), 0)
    col = lax.broadcasted_iota(jnp.int32, (64, 256), 1)
    pool = (col // STEPS == row).astype(BF16)
    lane = lax.broadcasted_iota(jnp.int32, (256, 128), 1)

    def rows(i, _):
        pl.when(i == 0)(toks[0].wait)
        pl.when(i == 1)(toks[1].wait)
        pl.when(i == 1)(toks[2].wait)
        squares[...] = jnp.zeros_like(squares)

        def colours(colour, _):
            for b, m in enumerate(ORDER):
                for c in range(2):
                    for h in range(2):
                        due = jnp.logical_and(i == 0, colour == c)
                        pl.when(due)(copies[2 * (4 * c + b) + h].wait)
                xs, ws, square = [], [], None
                for k in range(4):
                    ux, uy = user_of(colour, m, k)
                    at = pl.multiple_of((ux * 4 + uy) * 256 + colour * 128, 128)
                    x = tok[i, :, pl.ds(at, 128)]
                    wide = x.astype(F32)
                    square = wide * wide if square is None else square + wide * wide
                    xs.append(x)
                    ws.append(held[4 * colour + b, k])
                squares[...] += square
                d = jnp.dot(jnp.concatenate(xs, 1), jnp.concatenate(ws, 0), preferred_element_type=F32)
                if b == 0:
                    acc[...] = d + jnp.where(colour == 0, 0.0, acc[...])
                else:
                    acc[...] += d
            return 0

        lax.fori_loop(0, 2, colours, 0)
        scale = lax.rsqrt(jnp.sum(squares[...], axis=1, keepdims=True) / tok.shape[2] + 1e-05)
        for j in range(2):
            at = slice(j * 256, (j + 1) * 256)
            gate = acc[at, 0:384] * scale[at]
            up = acc[at, 384:768] * scale[at]
            mixed = acc[at, 768:896] * scale[at]
            hidden = (jax.nn.silu(gate) * up).astype(BF16)
            rest = jnp.where(lane < 64, jax.nn.silu(mixed) * pltpu.roll(mixed, 64, 1), 0.0).astype(BF16)
            hp = jnp.dot(pool, hidden, preferred_element_type=F32).astype(BF16)
            hp_rest = jnp.dot(pool, rest, preferred_element_type=F32).astype(BF16)
            for t in range(4):
                to = jnp.where(i == 0, place[j * 4 + t], place[8 + j * 4 + t])
                to = pl.ds(pl.multiple_of(to * 16, 16), 16)
                hp_ref[to, 0:384] = hp[t * 16 : (t + 1) * 16]
                hp_ref[to, 384:512] = hp_rest[t * 16 : (t + 1) * 16]
        return 0

    lax.fori_loop(0, 2, rows, 0)


def feed_forward(own, part, other, bundles):
    args = (own, part, other, *bundles)
    return pl.pallas_call(
        ff_kernel,
        out_shape=jax.ShapeDtypeStruct((256, 512), BF16),
        in_specs=[ANY] * len(args),
        out_specs=VMEM,
        scratch_shapes=[
            pltpu.VMEM((2, 512, own.shape[1]), BF16),
            pltpu.VMEM((512, 896), F32),
            pltpu.VMEM((512, 128), F32),
            pltpu.VMEM((2 * len(ORDER), 4, 128, 896), BF16),
            pltpu.SemaphoreType.DMA((4 * len(ORDER) + 3,)),
        ],
        name="feed_forward",
    )(*args)


def w2_kernel(spec, mine, theirs, *refs):
    bundles, out = refs[:-1], refs[-1]
    zl, core = lax.axis_index("zl"), lax.axis_index("core")
    acc = None
    for b, (colour, m) in enumerate(spec):
        ds, ps = [], []
        for k in range(4):
            ux, uy = user_of(colour, m, k)
            ds.append(jnp.concatenate([bundles[2 * b + k // 2][k % 2, :, j * 128 : (j + 1) * 128] for j in range(7)], 0))
            rel = lax.rem(ux - zl + 4, 4)
            col = pl.ds(pl.multiple_of((lax.rem(uy, 2) * 2 + colour) * 256, 256), 256)
            ps.append(jnp.where(uy // 2 == core, mine[rel, :, col], theirs[rel, :, col]))
        d = jnp.dot(jnp.concatenate(ds, 1), jnp.concatenate(ps, 0), preferred_element_type=F32)
        acc = d if acc is None else acc + d
    out[0:448, :] = acc.astype(BF16)
    out[448:512, :] = jnp.zeros((64, 256), BF16)


def down_proj(spec, mine, theirs, bundles):
    whole = pl.BlockSpec((4, 128, 1024), lambda i: (0, 0, 0))
    return pl.pallas_call(
        functools.partial(w2_kernel, spec),
        out_shape=jax.ShapeDtypeStruct((512, 256), BF16),
        grid=(1,),
        in_specs=[whole, whole] + [pl.BlockSpec((b.shape[0], 64, 896), lambda i: (0, 2, 0)) for b in bundles],
        out_specs=pl.BlockSpec((512, 256), lambda i: (0, 0)),
        name="down_proj",
    )(mine, theirs, *bundles)


def embed_kernel(hp, w0, w1, w2, w3, resid, keep, send, emb):
    y, core, zh = lax.axis_index("y"), lax.axis_index("core"), lax.axis_index("zh")
    for k, w in enumerate((w0, w1, w2, w3)):
        col = pl.ds(pl.multiple_of(lax.rem(y + k, 4) * 256, 256), 256)
        emb[:, col] = jnp.dot(hp[...], w[...], preferred_element_type=F32)
    half = pl.ds(pl.multiple_of(zh * 128, 128), 128)
    emb[half, :] += resid[...]
    for z in range(4):
        for c in range(2):
            at = pl.ds((z * 2 + c) * 16, 16)
            base = c * 128 + z * 32
            keep[at, :] = emb[pl.ds(pl.multiple_of(base + core * 16, 16), 16), :] * (1.0 / STEPS)
            send[at, :] = emb[pl.ds(pl.multiple_of(base + 16 - core * 16, 16), 16), :] * (1.0 / STEPS)


def embed(hp, parts, resid):
    shape = jax.ShapeDtypeStruct((128, 1024), F32)
    return pl.pallas_call(
        embed_kernel,
        out_shape=(shape, shape),
        in_specs=[VMEM] * 6,
        out_specs=(VMEM, VMEM),
        scratch_shapes=[pltpu.VMEM((256, 1024), F32)],
        name="embed",
    )(hp, *parts, resid)


def unit_rows(matrix):
    return (matrix * lax.rsqrt(jnp.sum(matrix * matrix, axis=1, keepdims=True) + 1e-06)).astype(BF16)


def candidate_kernel(parts, out):
    total = parts[0].astype(F32)
    for i in range(1, 8):
        total += parts[i].astype(F32)
    cand = unit_rows(total)
    for i in range(16):
        out[i] = cand


def candidates(parts):
    return pl.pallas_call(
        candidate_kernel,
        out_shape=jax.ShapeDtypeStruct((16, 16, 1024), BF16),
        in_specs=[VMEM],
        out_specs=VMEM,
        name="candidates",
    )(parts)


def row_of(k, s):
    core = lax.axis_index("core")
    core = core if s == 0 else 1 - core
    return lax.rem(lax.axis_index("zl") + k, 4) * 2 + core


def score_kernel(cands, mine, theirs, ids_row, ids_col, kernel_ref, note_ref, note):
    match = (ids_row[...] == ids_col[...]).astype(F32)
    count = jnp.sum(match, axis=0, keepdims=True)
    note[8:16, :] = jnp.broadcast_to(jnp.minimum(1.0, CAP / count), (8, 256))

    def block(k, _):
        for s, rows in enumerate((mine, theirs)):
            scores = lax.dot_general(
                cands[...], rows[k], (((1,), (1,)), ((), ())), preferred_element_type=F32
            )
            kernel = jnp.exp(scores * 60.0)
            kernel_ref[:, pl.ds(pl.multiple_of(s * 1024 + k * 256, 256), 256)] = kernel
            note[pl.ds(row_of(k, s), 1), :] = jnp.sum(kernel, axis=0, keepdims=True)
        return 0

    lax.fori_loop(0, 4, block, 0)
    for i in range(16):
        note_ref[i] = note[...]


def score(cands, mine, theirs, ids):
    return pl.pallas_call(
        score_kernel,
        out_shape=(
            jax.ShapeDtypeStruct((256, 2048), F32),
            jax.ShapeDtypeStruct((16, 16, 256), F32),
        ),
        in_specs=[VMEM] * 5,
        out_specs=(VMEM, VMEM),
        scratch_shapes=[pltpu.VMEM((16, 256), F32)],
        name="score",
    )(cands, mine, theirs, ids.reshape(1, 256), ids.reshape(256, 1))


def vote_kernel(notes, kernel, out, weight):
    totals = notes[0, 0:8, :]
    for i in range(1, 16):
        totals += notes[i, 0:8, :]
    for r in range(8):
        weight[r : r + 1, :] = notes[2 * r, 8:9, :] / totals[r : r + 1] * (4096 / 32768)
    acc = None
    for b in range(8):
        w = weight[pl.ds(row_of(b % 4, b // 4), 1), :]
        part = kernel[:, b * 256 : (b + 1) * 256] * w
        acc = part if acc is None else acc + part
    votes = jnp.sum(acc.T, axis=0, keepdims=True)
    pair = jnp.concatenate([votes[:, :128], votes[:, 128:]], 0)
    out[...] = jnp.broadcast_to(pair[None], (128, 2, 128))


def vote(notes, kernel):
    return pl.pallas_call(
        vote_kernel,
        out_shape=jax.ShapeDtypeStruct((128, 2, 128), F32),
        in_specs=[VMEM, VMEM],
        out_specs=VMEM,
        scratch_shapes=[pltpu.VMEM((8, 256), F32)],
        name="vote",
    )(notes, kernel)


def final_kernel(parts, out):
    lane = lax.broadcasted_iota(jnp.int32, (2, 128), 1)
    for g in range(8):
        total = parts[g * 16]
        for i in range(1, 16):
            total += parts[g * 16 + i]
        for r in range(8):
            moved = pltpu.roll(total, (g * 16 - r * 16) % 128, 1)
            here = jnp.logical_and(lane >= g * 16, lane < g * 16 + 16)
            old = out[:, r, :] if g > 0 else jnp.zeros((2, 128), F32)
            out[:, r, :] = jnp.where(here, moved, old)


def gather_votes(parts):
    return pl.pallas_call(
        final_kernel,
        out_shape=jax.ShapeDtypeStruct((2, 8, 128), F32),
        in_specs=[VMEM],
        out_specs=VMEM,
        name="gather_votes",
    )(parts)


ORDER = (0, 1, 3, 2)
BUNDLES = tuple((colour, m) for colour in range(2) for m in ORDER)


def shards(states, norm_gain, gate, up, down, proj, rows, enc, ids):
    zl, core, y = lax.axis_index("zl"), lax.axis_index("core"), lax.axis_index("y")
    a, b, piece = pack_weights(gate, up, down, norm_gain, states)
    q = send_z(piece, [(z, 7 - z) for z in range(8)])
    near_a = spread_first(a, "x")
    near_b = spread_first(b, "y")
    cols = lax.dynamic_slice_in_dim(proj, y * 256, 256, 1)
    cols = jnp.concatenate([cols[i * 128 : (i + 1) * 128] for i in range(4)], axis=1)
    near_cols = []
    for k in (-1, 2, 1):
        near_cols.append(shift_z(cols, k))
    a_lo, a_hi, b_lo, b_hi = stacks((a, near_a[0]), near_a[1:], (b, near_b[0]), near_b[1:])
    moves = [(a_lo, "y", 1), (a_hi, "y", -1), (b_lo, "x", 1), (b_hi, "x", -1)]
    moves += [(a_hi, "y", 1), (a_lo, "y", -1), (b_hi, "x", 1), (b_lo, "x", -1)]
    got = []
    for bundle, axis, k in moves:
        got.append(shift(bundle, axis, k))
    near = (a_lo, a_hi, got[5], got[1], got[0], got[4], b_lo, b_hi, got[7], got[3], got[2], got[6])
    part = exchange_states(states, q)
    pool = (jnp.arange(512)[None, :] // STEPS == jnp.arange(128)[:, None]).astype(BF16)
    state_cols = lax.dynamic_slice_in_dim(states, (zl * 2 + core) * 512, 512, 1)
    resid = jnp.dot(pool, state_cols, preferred_element_type=F32).astype(BF16)
    resid = jnp.dot(resid, proj, preferred_element_type=F32)
    encoded = unit_rows(jnp.dot(rows, enc, preferred_element_type=F32))
    (cols,) = stacks((cols, *near_cols))
    cols_other = swap_core(cols)
    far = []
    for i, (_, axis, k) in enumerate(moves[:4]):
        far.append(shift(got[i], axis, k))
    part, resid, encoded = lax.optimization_barrier((part, resid, encoded))
    other = swap_core(part)
    near_rows = []
    for k in (-1, 2, 1):
        near_rows.append(shift_z(encoded, k))
    bundles = near[:6] + tuple(far[:2]) + near[6:] + tuple(far[2:])
    w2 = down_proj(BUNDLES, cols, cols_other, bundles)
    parts = [w2]
    for k in (-1, 2, 1):
        parts.append(shift(w2, "y", k))
    hp = feed_forward(states, part, other, bundles)
    keep, send = embed(hp, parts, resid)
    emb = (keep + swap_core(send)).astype(BF16).reshape(8, 16, 1024)
    emb = lax.all_to_all(emb, ("zl", "zh"), 0, 0)
    cands, near = lax.optimization_barrier((candidates(emb), near_rows))
    (encoded,) = stacks((encoded, *near_rows))
    encoded_other = swap_core(encoded)
    cands = lax.all_to_all(cands, ("x", "y"), 0, 0).reshape(256, 1024)
    kernel, note = score(cands, encoded, encoded_other, ids)
    notes = lax.all_to_all(note, ("zl", "core", "zh"), 0, 0)
    partial = lax.all_to_all(vote(notes, kernel), ("zl", "core", "x", "y"), 0, 0)
    return gather_votes(partial).reshape(16, 1, 128)


def solution(mesh):
    fine = Mesh(mesh.devices.reshape(4, 2, 4, 4, 2), ("zl", "core", "x", "y", "zh"))
    gen, user, cand = ("zl", "core"), ("x", "y"), "zh"

    return jax.shard_map(
        shards,
        mesh=fine,
        in_specs=(
            P(user + (cand,), None),
            P(),
            P(user, gen),
            P(user, gen),
            P(gen, user),
            P(gen, None),
            P(gen + user, None),
            P(),
            P(gen + user),
        ),
        out_specs=P(None, cand, None),
        check_vma=False,
    )
```

```python
import functools

import functools

import jax
import jax.numpy as jnp
from jax import lax
from jax.experimental import pallas as pl
from jax.experimental.pallas import tpu as pltpu
from jax.sharding import Mesh, PartitionSpec as P

STEPS = 4
CAP = 8
F32 = jnp.float32
BF16 = jnp.bfloat16
VMEM = pl.BlockSpec(memory_space=pltpu.VMEM)
ANY = pl.BlockSpec(memory_space=pl.ANY)


def z_pairs(pairs):
    place = lambda z: (z % 4) * 2 + z // 4
    return [(place(a % 8), place(b % 8)) for a, b in pairs]


def shift_z(a, k):
    return lax.ppermute(a, ("zl", "zh"), z_pairs([(z, z + k) for z in range(8)]))


def send_z(a, pairs):
    return lax.ppermute(a, ("zl", "zh"), z_pairs(pairs))


def shift(a, axis, k):
    return lax.ppermute(a, axis, [(i, (i + k) % 4) for i in range(4)])


def swap_core(a):
    return lax.ppermute(a, "core", [(0, 1), (1, 0)])


def pack_kernel(gate, up, down, gain, states, out_a, out_b, piece, sem):
    c, zl, core = lax.axis_index("zh"), lax.axis_index("zl"), lax.axis_index("core")
    user = lax.axis_index("x") * 4 + lax.axis_index("y")
    start = pl.multiple_of((3 - zl) * 128 + core * 64, 64)
    copy = pltpu.make_async_copy(states.at[pl.ds(start, 64)], piece, sem)
    copy.start()
    full = pl.ds(pl.multiple_of(c * 512, 128), 384)
    lane = lax.broadcasted_iota(jnp.int32, (128, 128), 1)
    for i, out in enumerate((out_a, out_b)):
        at = slice(i * 128, (i + 1) * 128)
        scale = jnp.broadcast_to(gain[pl.ds(user * 2 + i, 1), :], (128, 128)).T
        wide = jnp.concatenate([scale] * 3, 1)
        out[0:128, 0:384] = (gate[at, full].astype(F32) * wide).astype(BF16)
        out[0:128, 384:768] = (up[at, full].astype(F32) * wide).astype(BF16)
        g = gate[at, 384:512].astype(F32)
        u = up[at, 384:512].astype(F32)
        g = jnp.where(c == 0, g, pltpu.roll(g, 64, 1))
        u = jnp.where(c == 0, pltpu.roll(u, 64, 1), u)
        out[0:128, 768:896] = (jnp.where(lane < 64, g, u) * scale).astype(BF16)
        for j in range(7):
            first = 384 + c * 64 if j == 6 else c * 512 + j * 64
            rows = pl.ds(pl.multiple_of(first, 64), 64)
            out[128:192, j * 128 : (j + 1) * 128] = down[rows, at]
    copy.wait()


def pack_weights(gate, up, down, gain, states):
    d = states.shape[1]
    return pl.pallas_call(
        pack_kernel,
        out_shape=(jax.ShapeDtypeStruct((192, 896), BF16),) * 2 + (jax.ShapeDtypeStruct((64, d), BF16),),
        in_specs=[VMEM] * 4 + [ANY],
        out_specs=(VMEM,) * 3,
        scratch_shapes=[pltpu.SemaphoreType.DMA],
        name="pack_weights",
    )(gate, up, down, gain.reshape(d // 128, 128), states)


def run_copies(copies):
    for copy in copies:
        copy.start()
    for copy in copies:
        copy.wait()


def stack_kernel(groups, *refs):
    n = sum(groups)
    ins, outs, sems = refs[:n], refs[n:-1], refs[-1]
    copies, at = [], 0
    for size, out in zip(groups, outs):
        for k in range(size):
            copies.append(pltpu.make_async_copy(ins[at], out.at[k], sems.at[at]))
            at += 1
    run_copies(copies)


def stacks(*groups):
    arrays = [a for group in groups for a in group]
    out = tuple(jax.ShapeDtypeStruct((len(g),) + g[0].shape, g[0].dtype) for g in groups)
    return pl.pallas_call(
        functools.partial(stack_kernel, tuple(len(g) for g in groups)),
        out_shape=out,
        in_specs=[ANY] * len(arrays),
        out_specs=(VMEM,) * len(groups),
        scratch_shapes=[pltpu.SemaphoreType.DMA((len(arrays),))],
        name="stacks",
    )(*arrays)


def spread_first(chunk, axis):
    got = []
    for k in (-1, 2, 1):
        got.append(shift(chunk, axis, k))
    return got


def relay_kernel(states, q, *refs):
    outs, sems = refs[:4], refs[4]
    zl, core = lax.axis_index("zl"), lax.axis_index("core")
    for i, (out, end, piece) in enumerate(zip(outs, (3, 0, 3, 0), (2, 1, 3, 0))):
        own = states.at[pl.ds(pl.multiple_of(piece * 128 + core * 64, 64), 64)]
        pl.when(zl == end)(pltpu.make_async_copy(own, out, sems.at[i]).start)
        pl.when(zl != end)(pltpu.make_async_copy(q, out, sems.at[i]).start)
    for i, out in enumerate(outs):
        pltpu.make_async_copy(q, out, sems.at[i]).wait()


def join_kernel(q, p1, p2, p3, p4, out, sems):
    zl = lax.axis_index("zl")
    for i, p in enumerate((q, p1, p2)):
        pltpu.make_async_copy(p, out.at[pl.ds(i * 64, 64)], sems.at[i]).start()
    to = out.at[pl.ds(192, 64)]
    even = lax.rem(zl, 2) == 0
    pl.when(even)(pltpu.make_async_copy(p3, to, sems.at[3]).start)
    pl.when(jnp.logical_not(even))(pltpu.make_async_copy(p4, to, sems.at[3]).start)
    for i in range(4):
        pltpu.make_async_copy(q, out.at[pl.ds(i * 64, 64)], sems.at[i]).wait()


def exchange_states(states, q):
    sent = jax.ShapeDtypeStruct(q.shape, q.dtype)
    up, dn, up2, dn2 = pl.pallas_call(
        relay_kernel,
        out_shape=(sent,) * 4,
        in_specs=[ANY] * 2,
        out_specs=(VMEM,) * 4,
        scratch_shapes=[pltpu.SemaphoreType.DMA((4,))],
        name="relay",
    )(states, q)
    p1 = shift_z(up, 1)
    p2 = shift_z(dn, -1)
    p3 = send_z(up2, [(0, 2), (4, 6), (3, 4), (7, 0)])
    p4 = send_z(dn2, [(3, 1), (7, 5), (0, 7), (4, 3)])
    return pl.pallas_call(
        join_kernel,
        out_shape=jax.ShapeDtypeStruct((256, q.shape[1]), q.dtype),
        in_specs=[ANY] * 5,
        out_specs=VMEM,
        scratch_shapes=[pltpu.SemaphoreType.DMA((4,))],
        name="join",
    )(q, p1, p2, p3, p4)


def places():
    zl, core, c = lax.axis_index("zl"), lax.axis_index("core"), lax.axis_index("zh")
    pieces = (
        zl,
        jnp.where(zl == 0, 2, zl - 1),
        jnp.where(zl == 3, 1, zl + 1),
        jnp.where(zl < 2, 3, 0),
    )
    own = [c * 8 + i for i in range(8)]
    part = [(1 - c) * 8 + p * 2 + core for p in pieces]
    other = [(1 - c) * 8 + p * 2 + 1 - core for p in pieces]
    return own + part + other


def user_of(colour, m, k):
    x, y = lax.axis_index("x"), lax.axis_index("y")
    if isinstance(colour, int):
        dx, dy = (k, m) if colour == 0 else (m, k)
    else:
        dx, dy = jnp.where(colour == 0, k, m), jnp.where(colour == 0, m, k)
    return lax.rem(x + dx, 4), lax.rem(y + dy, 4)


def ff_kernel(own, part, other, *refs):
    n = 4 * len(ORDER)
    bundles, refs = refs[:n], refs[n:]
    hp_ref, tok, acc, squares, held, sems = refs
    copies = [
        pltpu.make_async_copy(b.at[:, pl.ds(0, 128)], held.at[i // 2, pl.ds(i % 2 * 2, 2)], sems.at[i])
        for i, b in enumerate(bundles)
    ]
    toks = [
        pltpu.make_async_copy(own, tok.at[0], sems.at[n]),
        pltpu.make_async_copy(part, tok.at[1, pl.ds(0, 256)], sems.at[n + 1]),
        pltpu.make_async_copy(other, tok.at[1, pl.ds(256, 256)], sems.at[n + 2]),
    ]
    toks[0].start()
    for copy in copies + toks[1:]:
        copy.start()
    place = places()
    row = lax.broadcasted_iota(jnp.int32, (64, 256), 0)
    col = lax.broadcasted_iota(jnp.int32, (64, 256), 1)
    pool = (col // STEPS == row).astype(BF16)
    lane = lax.broadcasted_iota(jnp.int32, (256, 128), 1)

    def rows(i, _):
        pl.when(i == 0)(toks[0].wait)
        pl.when(i == 1)(toks[1].wait)
        pl.when(i == 1)(toks[2].wait)
        squares[...] = jnp.zeros_like(squares)

        def colours(colour, _):
            for b, m in enumerate(ORDER):
                for c in range(2):
                    for h in range(2):
                        due = jnp.logical_and(i == 0, colour == c)
                        pl.when(due)(copies[2 * (4 * c + b) + h].wait)
                xs, ws, square = [], [], None
                for k in range(4):
                    ux, uy = user_of(colour, m, k)
                    at = pl.multiple_of((ux * 4 + uy) * 256 + colour * 128, 128)
                    x = tok[i, :, pl.ds(at, 128)]
                    wide = x.astype(F32)
                    square = wide * wide if square is None else square + wide * wide
                    xs.append(x)
                    ws.append(held[4 * colour + b, k])
                squares[...] += square
                d = jnp.dot(jnp.concatenate(xs, 1), jnp.concatenate(ws, 0), preferred_element_type=F32)
                if b == 0:
                    acc[...] = d + jnp.where(colour == 0, 0.0, acc[...])
                else:
                    acc[...] += d
            return 0

        lax.fori_loop(0, 2, colours, 0)
        scale = lax.rsqrt(jnp.sum(squares[...], axis=1, keepdims=True) / tok.shape[2] + 1e-05)
        for j in range(2):
            at = slice(j * 256, (j + 1) * 256)
            gate = acc[at, 0:384] * scale[at]
            up = acc[at, 384:768] * scale[at]
            mixed = acc[at, 768:896] * scale[at]
            hidden = (jax.nn.silu(gate) * up).astype(BF16)
            rest = jnp.where(lane < 64, jax.nn.silu(mixed) * pltpu.roll(mixed, 64, 1), 0.0).astype(BF16)
            hp = jnp.dot(pool, hidden, preferred_element_type=F32).astype(BF16)
            hp_rest = jnp.dot(pool, rest, preferred_element_type=F32).astype(BF16)
            for t in range(4):
                to = jnp.where(i == 0, place[j * 4 + t], place[8 + j * 4 + t])
                to = pl.ds(pl.multiple_of(to * 16, 16), 16)
                hp_ref[to, 0:384] = hp[t * 16 : (t + 1) * 16]
                hp_ref[to, 384:512] = hp_rest[t * 16 : (t + 1) * 16]
        return 0

    lax.fori_loop(0, 2, rows, 0)


def feed_forward(own, part, other, bundles):
    args = (own, part, other, *bundles)
    return pl.pallas_call(
        ff_kernel,
        out_shape=jax.ShapeDtypeStruct((256, 512), BF16),
        in_specs=[ANY] * len(args),
        out_specs=VMEM,
        scratch_shapes=[
            pltpu.VMEM((2, 512, own.shape[1]), BF16),
            pltpu.VMEM((512, 896), F32),
            pltpu.VMEM((512, 128), F32),
            pltpu.VMEM((2 * len(ORDER), 4, 128, 896), BF16),
            pltpu.SemaphoreType.DMA((4 * len(ORDER) + 3,)),
        ],
        name="feed_forward",
    )(*args)


def w2_kernel(spec, mine, theirs, *refs):
    bundles, out = refs[:-1], refs[-1]
    zl, core = lax.axis_index("zl"), lax.axis_index("core")
    acc = None
    for b, (colour, m) in enumerate(spec):
        ds, ps = [], []
        for k in range(4):
            ux, uy = user_of(colour, m, k)
            ds.append(jnp.concatenate([bundles[2 * b + k // 2][k % 2, :, j * 128 : (j + 1) * 128] for j in range(7)], 0))
            rel = lax.rem(ux - zl + 4, 4)
            col = pl.ds(pl.multiple_of((lax.rem(uy, 2) * 2 + colour) * 256, 256), 256)
            ps.append(jnp.where(uy // 2 == core, mine[rel, :, col], theirs[rel, :, col]))
        d = jnp.dot(jnp.concatenate(ds, 1), jnp.concatenate(ps, 0), preferred_element_type=F32)
        acc = d if acc is None else acc + d
    out[0:448, :] = acc.astype(BF16)
    out[448:512, :] = jnp.zeros((64, 256), BF16)


def down_proj(spec, mine, theirs, bundles):
    whole = pl.BlockSpec((4, 128, 1024), lambda i: (0, 0, 0))
    return pl.pallas_call(
        functools.partial(w2_kernel, spec),
        out_shape=jax.ShapeDtypeStruct((512, 256), BF16),
        grid=(1,),
        in_specs=[whole, whole] + [pl.BlockSpec((b.shape[0], 64, 896), lambda i: (0, 2, 0)) for b in bundles],
        out_specs=pl.BlockSpec((512, 256), lambda i: (0, 0)),
        name="down_proj",
    )(mine, theirs, *bundles)


def embed_kernel(hp, w0, w1, w2, w3, resid, keep, send, emb):
    y, core, zh = lax.axis_index("y"), lax.axis_index("core"), lax.axis_index("zh")
    for k, w in enumerate((w0, w1, w2, w3)):
        col = pl.ds(pl.multiple_of(lax.rem(y + k, 4) * 256, 256), 256)
        emb[:, col] = jnp.dot(hp[...], w[...], preferred_element_type=F32)
    half = pl.ds(pl.multiple_of(zh * 128, 128), 128)
    emb[half, :] += resid[...]
    for z in range(4):
        for c in range(2):
            at = pl.ds((z * 2 + c) * 16, 16)
            base = c * 128 + z * 32
            keep[at, :] = emb[pl.ds(pl.multiple_of(base + core * 16, 16), 16), :] * (1.0 / STEPS)
            send[at, :] = emb[pl.ds(pl.multiple_of(base + 16 - core * 16, 16), 16), :] * (1.0 / STEPS)


def embed(hp, parts, resid):
    shape = jax.ShapeDtypeStruct((128, 1024), F32)
    return pl.pallas_call(
        embed_kernel,
        out_shape=(shape, shape),
        in_specs=[VMEM] * 6,
        out_specs=(VMEM, VMEM),
        scratch_shapes=[pltpu.VMEM((256, 1024), F32)],
        name="embed",
    )(hp, *parts, resid)


def unit_rows(matrix):
    return (matrix * lax.rsqrt(jnp.sum(matrix * matrix, axis=1, keepdims=True) + 1e-06)).astype(BF16)


def encode_kernel(rows, enc, out):
    out[...] = unit_rows(jnp.dot(rows[...], enc[...], preferred_element_type=F32))


def encode(rows, enc):
    n, d = rows.shape
    return pl.pallas_call(
        encode_kernel,
        out_shape=jax.ShapeDtypeStruct((n, enc.shape[1]), BF16),
        grid=(2,),
        in_specs=[
            pl.BlockSpec((n // 2, d), lambda i: (i, 0)),
            pl.BlockSpec(enc.shape, lambda i: (0, 0)),
        ],
        out_specs=pl.BlockSpec((n // 2, enc.shape[1]), lambda i: (i, 0)),
        name="encode",
    )(rows, enc)


def candidate_kernel(parts, out):
    total = parts[0].astype(F32)
    for i in range(1, 8):
        total += parts[i].astype(F32)
    cand = unit_rows(total)
    for i in range(16):
        out[i] = cand


def candidates(parts):
    return pl.pallas_call(
        candidate_kernel,
        out_shape=jax.ShapeDtypeStruct((16, 16, 1024), BF16),
        in_specs=[VMEM],
        out_specs=VMEM,
        name="candidates",
    )(parts)


def row_of(k, s):
    core = lax.axis_index("core")
    core = core if s == 0 else 1 - core
    return lax.rem(lax.axis_index("zl") + k, 4) * 2 + core


def score_kernel(cands, mine, theirs, ids_row, ids_col, kernel_ref, note_ref, note):
    match = (ids_row[...] == ids_col[...]).astype(F32)
    count = jnp.sum(match, axis=0, keepdims=True)
    note[8:16, :] = jnp.broadcast_to(jnp.minimum(1.0, CAP / count), (8, 256))

    def block(k, _):
        for s, rows in enumerate((mine, theirs)):
            scores = lax.dot_general(
                cands[...], rows[k], (((1,), (1,)), ((), ())), preferred_element_type=F32
            )
            kernel = jnp.exp(scores * 60.0)
            kernel_ref[:, pl.ds(pl.multiple_of(s * 1024 + k * 256, 256), 256)] = kernel
            note[pl.ds(row_of(k, s), 1), :] = jnp.sum(kernel, axis=0, keepdims=True)
        return 0

    lax.fori_loop(0, 4, block, 0)
    for i in range(16):
        note_ref[i] = note[...]


def score(cands, mine, theirs, ids):
    return pl.pallas_call(
        score_kernel,
        out_shape=(
            jax.ShapeDtypeStruct((256, 2048), F32),
            jax.ShapeDtypeStruct((16, 16, 256), F32),
        ),
        in_specs=[VMEM] * 5,
        out_specs=(VMEM, VMEM),
        scratch_shapes=[pltpu.VMEM((16, 256), F32)],
        name="score",
    )(cands, mine, theirs, ids.reshape(1, 256), ids.reshape(256, 1))


def vote_kernel(notes, kernel, out, weight):
    totals = notes[0, 0:8, :]
    for i in range(1, 16):
        totals += notes[i, 0:8, :]
    for r in range(8):
        weight[r : r + 1, :] = notes[2 * r, 8:9, :] / totals[r : r + 1] * (4096 / 32768)
    acc = None
    for b in range(8):
        w = weight[pl.ds(row_of(b % 4, b // 4), 1), :]
        part = kernel[:, b * 256 : (b + 1) * 256] * w
        acc = part if acc is None else acc + part
    votes = jnp.sum(acc.T, axis=0, keepdims=True)
    pair = jnp.concatenate([votes[:, :128], votes[:, 128:]], 0)
    out[...] = jnp.broadcast_to(pair[None], (128, 2, 128))


def vote(notes, kernel):
    return pl.pallas_call(
        vote_kernel,
        out_shape=jax.ShapeDtypeStruct((128, 2, 128), F32),
        in_specs=[VMEM, VMEM],
        out_specs=VMEM,
        scratch_shapes=[pltpu.VMEM((8, 256), F32)],
        name="vote",
    )(notes, kernel)


def final_kernel(parts, out):
    lane = lax.broadcasted_iota(jnp.int32, (2, 128), 1)
    for g in range(8):
        total = parts[g * 16]
        for i in range(1, 16):
            total += parts[g * 16 + i]
        for r in range(8):
            moved = pltpu.roll(total, (g * 16 - r * 16) % 128, 1)
            here = jnp.logical_and(lane >= g * 16, lane < g * 16 + 16)
            old = out[:, r, :] if g > 0 else jnp.zeros((2, 128), F32)
            out[:, r, :] = jnp.where(here, moved, old)


def gather_votes(parts):
    return pl.pallas_call(
        final_kernel,
        out_shape=jax.ShapeDtypeStruct((2, 8, 128), F32),
        in_specs=[VMEM],
        out_specs=VMEM,
        name="gather_votes",
    )(parts)


ORDER = (0, 1, 3, 2)
BUNDLES = tuple((colour, m) for colour in range(2) for m in ORDER)


def shards(states, norm_gain, gate, up, down, proj, rows, enc, ids):
    zl, core, y = lax.axis_index("zl"), lax.axis_index("core"), lax.axis_index("y")
    a, b, piece = pack_weights(gate, up, down, norm_gain, states)
    q = send_z(piece, [(z, 7 - z) for z in range(8)])
    near_a = spread_first(a, "x")
    near_b = spread_first(b, "y")
    cols = lax.dynamic_slice_in_dim(proj, y * 256, 256, 1)
    cols = jnp.concatenate([cols[i * 128 : (i + 1) * 128] for i in range(4)], axis=1)
    near_cols = []
    for k in (-1, 2, 1):
        near_cols.append(shift_z(cols, k))
    a_lo, a_hi, b_lo, b_hi = stacks((a, near_a[0]), near_a[1:], (b, near_b[0]), near_b[1:])
    moves = [(a_lo, "y", 1), (a_hi, "y", -1), (b_lo, "x", 1), (b_hi, "x", -1)]
    moves += [(a_hi, "y", 1), (a_lo, "y", -1), (b_hi, "x", 1), (b_lo, "x", -1)]
    got = []
    for bundle, axis, k in moves:
        got.append(shift(bundle, axis, k))
    near = (a_lo, a_hi, got[5], got[1], got[0], got[4], b_lo, b_hi, got[7], got[3], got[2], got[6])
    part = exchange_states(states, q)
    pool = (jnp.arange(512)[None, :] // STEPS == jnp.arange(128)[:, None]).astype(BF16)
    state_cols = lax.dynamic_slice_in_dim(states, (zl * 2 + core) * 512, 512, 1)
    resid = jnp.dot(pool, state_cols, preferred_element_type=F32).astype(BF16)
    resid = jnp.dot(resid, proj, preferred_element_type=F32)
    encoded = encode(rows, enc)
    (cols,) = stacks((cols, *near_cols))
    cols_other = swap_core(cols)
    far = []
    for i, (_, axis, k) in enumerate(moves[:4]):
        far.append(shift(got[i], axis, k))
    part, resid, encoded = lax.optimization_barrier((part, resid, encoded))
    other = swap_core(part)
    near_rows = []
    for k in (-1, 2, 1):
        near_rows.append(shift_z(encoded, k))
    bundles = near[:6] + tuple(far[:2]) + near[6:] + tuple(far[2:])
    w2 = down_proj(BUNDLES, cols, cols_other, bundles)
    parts = [w2]
    for k in (-1, 2, 1):
        parts.append(shift(w2, "y", k))
    hp = feed_forward(states, part, other, bundles)
    keep, send = embed(hp, parts, resid)
    emb = (keep + swap_core(send)).astype(BF16).reshape(8, 16, 1024)
    emb = lax.all_to_all(emb, ("zl", "zh"), 0, 0)
    cands, near = lax.optimization_barrier((candidates(emb), near_rows))
    (encoded,) = stacks((encoded, *near_rows))
    encoded_other = swap_core(encoded)
    cands = lax.all_to_all(cands, ("x", "y"), 0, 0).reshape(256, 1024)
    kernel, note = score(cands, encoded, encoded_other, ids)
    notes = lax.all_to_all(note, ("zl", "core", "zh"), 0, 0)
    partial = lax.all_to_all(vote(notes, kernel), ("zl", "core", "x", "y"), 0, 0)
    return gather_votes(partial).reshape(16, 1, 128)


def solution(mesh):
    fine = Mesh(mesh.devices.reshape(4, 2, 4, 4, 2), ("zl", "core", "x", "y", "zh"))
    gen, user, cand = ("zl", "core"), ("x", "y"), "zh"

    return jax.shard_map(
        shards,
        mesh=fine,
        in_specs=(
            P(user + (cand,), None),
            P(),
            P(user, gen),
            P(user, gen),
            P(gen, user),
            P(gen, None),
            P(gen + user, None),
            P(),
            P(gen + user),
        ),
        out_specs=P(None, cand, None),
        check_vma=False,
    )
```
